256 devices in a mesh: blk: 256 (over y, z, x, core).
Axes of the slice: x: 4, y: 4, z: 8, core: 2. Of those that a mesh axis runs over, the one named last changes fastest.
Arguments:
- state: float32 [768, 6, 16, 256], P('blk'), may hold values from -0.5 to 3, as said below
- wall_dist: float32 [768, 16, 256], P('blk'), may hold values from 0.2 to 2
- block_metric: float32 [768, 10], P('blk'), may hold values from -1 to 1
- inflow: float32 [6], replicated, may hold values from 0.5 to 1
- counts: int32 [256], P('blk'), may hold values from 1 to 3, as said below
- links: int32 [768, 6, 4], P('blk'), may hold values from 0 to 767, as said below
Outputs:
- tendency: float32 [768, 6, 16, 256], P('blk')
- time_step: float32 [], replicated
The draws below stay inside these ranges and needn't reach their ends.
Inputs may be any that keep to these rules, and one draw needn't show every extreme that they name: `state`: field 0 lies in 0.8 to 1.2, fields 1 to 3 in -0.5 to 0.5, field 4 in 2 to 3, field 5 in 0 to 0.4. `counts`: every device has 1 to 3 blocks in use, in its first slots; some device has 3. `links`: code 3 marks an interface, 0 far field, 1 wall, 2 outflow. Interfaces join blocks in use and are mutual: if face f of b names face h of g with orientation o, then face h of g names face f of b with the inverse reindexing. i faces pair with i faces (any o of 0 to 7); j and k faces pair with j or k faces, with o even. A partner block lies on a device whose index differs by at most 2 along the axis, counted cyclically. Of the faces of one device, at most 1 i face and at most 3 j or k faces name blocks on any one other device, and some device has 3 j or k faces naming blocks of one other device. For boundary faces and unused slots the partner is the block itself.
All inputs are finite; a program needn't handle non-finite values.
Results may differ from the reference program's by a relative error of at most 0.0003.
Values sent between devices are 32-bit elements; how exact they have to be, the bound alone decides.
No kernel may reach another device: no remote copies, remote signals or barrier semaphores. Data moves between devices by JAX's collectives and lax.ppermute only.
A program may use at most 128 MiB of HBM per device.

```python
import math
import jax
import jax.numpy as jnp
from jax import lax

NI = 16
NJ = 16
NK = 16
SLOTS = 3
BLK_ALL = 768


def draw_state(key, part):
    keys = jax.random.split(jax.random.fold_in(key, 311), 4)
    shape = (BLK_ALL, NI, NJ * NK)
    density = jax.random.uniform(keys[0], shape, jnp.float32, 0.8, 1.2)
    momentum = jax.random.uniform(keys[1], (3,) + shape, jnp.float32, -0.5, 0.5)
    energy = jax.random.uniform(keys[2], shape, jnp.float32, 2.0, 3.0)
    nu_tilde = jax.random.uniform(keys[3], shape, jnp.float32, 0.02, 0.3)
    stacked = jnp.concatenate([density[None], momentum, energy[None], (density * nu_tilde)[None]], axis=0)
    return jnp.transpose(stacked, (1, 0, 2, 3))


def invert_orient(orient):
    swapped = orient % 2
    first_rev = orient // 2 % 2
    second_rev = orient // 4 % 2
    return swapped + 2 * jnp.where(swapped == 1, second_rev, first_rev) + 4 * jnp.where(swapped == 1, first_rev, second_rev)


def connect(key):
    dev_count = BLK_ALL // SLOTS
    keys = jax.random.split(jax.random.fold_in(key, 7171), 8)
    level = jax.random.randint(keys[0], (dev_count,), 0, 10)
    counts = jnp.where(level < 6, 1, jnp.where(level < 8, min(2, SLOTS), SLOTS)).astype(jnp.int32)
    heavy = jax.random.randint(keys[1], (), 0, dev_count)
    counts = counts.at[heavy].set(SLOTS)
    counts = counts.at[(heavy + 1) % dev_count].set(SLOTS)
    block_ids = jnp.arange(BLK_ALL, dtype=jnp.int32)
    in_use = block_ids % SLOTS < counts[block_ids // SLOTS]
    rank = jnp.cumsum(in_use.astype(jnp.int32)) - 1
    total = jnp.sum(in_use.astype(jnp.int32))
    score = jnp.where(in_use, block_ids, BLK_ALL + block_ids)
    ordered = jnp.argsort(score, stable=True).astype(jnp.int32)

    def moved(delta):
        return ordered[(rank + delta + 2 * total) % total]
    next_one, next_two, prev_one, prev_two = (moved(1), moved(2), moved(-1), moved(-2))
    orient_i = jax.random.randint(keys[2], (BLK_ALL,), 0, 8)
    orient_j = 2 * jax.random.randint(keys[3], (BLK_ALL,), 0, 4)
    orient_k = 2 * jax.random.randint(keys[4], (BLK_ALL,), 0, 4)
    k_joined = jax.random.randint(keys[5], (BLK_ALL,), 0, 2)
    k_joined = k_joined.at[heavy * SLOTS + SLOTS - 1].set(1)
    code_low = jax.random.randint(keys[6], (BLK_ALL,), 0, 3)
    code_high = jax.random.randint(keys[7], (BLK_ALL,), 0, 3)
    three = jnp.full((BLK_ALL,), 3, jnp.int32)
    zeros = jnp.zeros((BLK_ALL,), jnp.int32)
    face_lo_i = jnp.stack([three, prev_one, zeros + 1, invert_orient(orient_i[prev_one])], -1)
    face_hi_i = jnp.stack([three, next_one, zeros, orient_i], -1)
    face_lo_j = jnp.stack([three, prev_two, zeros + 3, orient_j[prev_two]], -1)
    face_hi_j = jnp.stack([three, next_two, zeros + 2, orient_j], -1)
    lo_join = k_joined[prev_one] == 1
    face_lo_k = jnp.where(lo_join[:, None], jnp.stack([three, prev_one, zeros + 5, orient_k[prev_one]], -1), jnp.stack([code_low, block_ids, zeros + 4, zeros], -1))
    face_hi_k = jnp.where((k_joined == 1)[:, None], jnp.stack([three, next_one, zeros + 4, orient_k], -1), jnp.stack([code_high, block_ids, zeros + 5, zeros], -1))
    links = jnp.stack([face_lo_i, face_hi_i, face_lo_j, face_hi_j, face_lo_k, face_hi_k], 1)
    face_nums = jnp.arange(6, dtype=jnp.int32)
    spare_rows = jnp.stack([jnp.full((BLK_ALL, 6), 2, jnp.int32), jnp.broadcast_to(block_ids[:, None], (BLK_ALL, 6)), jnp.broadcast_to(face_nums[None, :], (BLK_ALL, 6)), jnp.zeros((BLK_ALL, 6), jnp.int32)], -1)
    links = jnp.where(in_use[:, None, None], links, spare_rows).astype(jnp.int32)
    return (counts, links)


def draw_counts(key, part):
    return connect(key)[0]


def draw_links(key, part):
    return connect(key)[1]


def level_of(stream_key, shape, pieces, low, largest):
    level, own = 1.0, jax.random.fold_in(stream_key, 6)
    for axis_at, shards_of in pieces:
        heights = jnp.exp(jax.random.uniform(jax.random.fold_in(own, axis_at), (shards_of,), jnp.float32, low / len(pieces), largest / len(pieces)))
        level = level * jnp.repeat(heights, shape[axis_at] // shards_of).reshape([-1 if axis == axis_at else 1 for axis in range(len(shape))])
    return level


def setup_inputs(seed: int = 0) -> dict:
    arg_keys = jax.random.split(jax.random.key(seed), 7)
    return {
        "state": draw_state(jax.random.fold_in(arg_keys[6], 71), 0),
        "wall_dist": jnp.clip(jnp.exp(math.log(2.0) - 2.3025851 * jax.random.uniform(arg_keys[1], (BLK_ALL, NI, NJ * NK), jnp.float32) ** level_of(arg_keys[1], (BLK_ALL, NI, NJ * NK), ((0, 256),), -0.2, 0.2)), 0.2, 2.0),
        "block_metric": jnp.clip(jax.random.uniform(arg_keys[2], (BLK_ALL, 10), jnp.float32, -1.0, 1.0) * level_of(arg_keys[2], (BLK_ALL, 10), ((0, 256),), -0.4, 0.0), -1.0, 1.0),
        "inflow": jnp.clip(jax.random.uniform(arg_keys[3], (6,), jnp.float32, 0.5, 1.0), 0.5, 1.0),
        "counts": draw_counts(jax.random.fold_in(arg_keys[6], 71), 0),
        "links": draw_links(jax.random.fold_in(arg_keys[6], 71), 0),
    }


GAMMA = 1.4
PROD_COEF = 0.1355
DEST_COEF = 3.239
COURANT = 0.5
WALL_SIGNS = (1.0, -1.0, -1.0, -1.0, 1.0, -1.0)

def point_flux(conserved, normal):
    density = conserved[0]
    velocity = conserved[1:4] / density
    pressure = (GAMMA - 1.0) * (conserved[4] - 0.5 * density * lax.optimization_barrier(jnp.sum(velocity * velocity, axis=0)))
    normal_vel = normal[0] * velocity[0] + normal[1] * velocity[1] + normal[2] * velocity[2]
    face_area = jnp.sqrt(jnp.sum(normal * normal))
    sound_speed = jnp.sqrt(GAMMA * pressure / density)
    fluxes = jnp.stack([conserved[0] * normal_vel, conserved[1] * normal_vel + pressure * normal[0], conserved[2] * normal_vel + pressure * normal[1], conserved[3] * normal_vel + pressure * normal[2], (conserved[4] + pressure) * normal_vel, conserved[5] * normal_vel])
    speeds = jnp.abs(normal_vel) + sound_speed * face_area
    return (fluxes, speeds)

def cell_index():
    flat_index = jnp.arange(NJ * NK, dtype=jnp.int32)
    return (flat_index // NK, flat_index % NK)

def shift_up(values, ghost_layer, axis_dir):
    if axis_dir == 0:
        return jnp.concatenate([values[..., 1:, :], ghost_layer[..., None, :]], axis=-2)
    j_index, k_index = cell_index()
    if axis_dir == 1:
        shifted = jnp.concatenate([values[..., NK:], jnp.zeros_like(values[..., :NK])], axis=-1)
        placed = jnp.tile(ghost_layer, (1,) * (ghost_layer.ndim - 1) + (NJ,))
        return jnp.where(j_index == NJ - 1, placed, shifted)
    shifted = jnp.concatenate([values[..., 1:], jnp.zeros_like(values[..., :1])], axis=-1)
    placed = jnp.repeat(ghost_layer, NK, axis=-1)
    return jnp.where(k_index == NK - 1, placed, shifted)

def shift_down(values, ghost_layer, axis_dir):
    if axis_dir == 0:
        return jnp.concatenate([ghost_layer[..., None, :], values[..., :-1, :]], axis=-2)
    j_index, k_index = cell_index()
    if axis_dir == 1:
        shifted = jnp.concatenate([jnp.zeros_like(values[..., :NK]), values[..., :-NK]], axis=-1)
        placed = jnp.tile(ghost_layer, (1,) * (ghost_layer.ndim - 1) + (NJ,))
        return jnp.where(j_index == 0, placed, shifted)
    shifted = jnp.concatenate([jnp.zeros_like(values[..., :1]), values[..., :-1]], axis=-1)
    placed = jnp.repeat(ghost_layer, NK, axis=-1)
    return jnp.where(k_index == 0, placed, shifted)

def first_slab(values, axis_dir):
    if axis_dir == 0:
        return values[..., 0, :]
    if axis_dir == 1:
        return values[..., :NK]
    return values.reshape(values.shape[:-1] + (NJ, NK))[..., 0]

def last_slab(values, axis_dir):
    if axis_dir == 0:
        return values[..., -1, :]
    if axis_dir == 1:
        return values[..., NJ * NK - NK:]
    return values.reshape(values.shape[:-1] + (NJ, NK))[..., NK - 1]

def block_faces(conserved):
    faces_i = jnp.stack([first_slab(conserved, 0), last_slab(conserved, 0)])
    faces_jk = jnp.stack([first_slab(conserved, 1).reshape(6, -1), last_slab(conserved, 1).reshape(6, -1), first_slab(conserved, 2).reshape(6, -1), last_slab(conserved, 2).reshape(6, -1)])
    return (faces_i, faces_jk)

def inflow_state(inflow):
    density = inflow[0]
    velocity = inflow[1:4]
    energy = inflow[4] / (GAMMA - 1.0) + 0.5 * density * jnp.sum(velocity * velocity)
    return jnp.stack([density, density * velocity[0], density * velocity[1], density * velocity[2], energy, density * inflow[5]])

def make_ghost(partner_layer, own_layer, face_code, orient, square):
    if square:
        layer_grid = partner_layer.reshape(6, NJ, NK)
        layer_grid = jnp.where(orient % 2 == 1, jnp.swapaxes(layer_grid, 1, 2), layer_grid)
    else:
        layer_grid = partner_layer.reshape(6, NI, NK)
    layer_grid = jnp.where(orient // 2 % 2 == 1, jnp.flip(layer_grid, 1), layer_grid)
    layer_grid = jnp.where(orient // 4 % 2 == 1, jnp.flip(layer_grid, 2), layer_grid)
    return layer_grid.reshape(6, -1)

def finish_ghost(oriented, own_layer, face_code, inflow_cons):
    wall_signs = jnp.array(WALL_SIGNS, dtype=jnp.float32)[:, None]
    wall_layer = own_layer * wall_signs
    far_layer = jnp.broadcast_to(inflow_cons[:, None], own_layer.shape)
    return jnp.where(face_code == 3, oriented, jnp.where(face_code == 0, far_layer, jnp.where(face_code == 1, wall_layer, own_layer)))

def block_rate(conserved, ghosts, metric_row, distance):
    normals = jnp.eye(3, dtype=jnp.float32) + 0.25 * metric_row[:9].reshape(3, 3)
    volume = 1.0 + 0.25 * metric_row[9]
    shapes = ((6, NJ * NK), (6, NI, NK), (6, NI, NJ))
    net_flux = jnp.zeros_like(conserved)
    speed_sum = jnp.zeros_like(distance)
    vel_diffs = []
    for axis_dir in range(3):
        normal = normals[axis_dir]
        lower_ghost = ghosts[2 * axis_dir].reshape(shapes[axis_dir])
        upper_ghost = ghosts[2 * axis_dir + 1].reshape(shapes[axis_dir])
        fluxes, speeds = point_flux(conserved, normal)
        up_flux, up_speed = point_flux(upper_ghost, normal)
        low_flux, low_speed = point_flux(lower_ghost, normal)
        above_cells = shift_up(conserved, upper_ghost, axis_dir)
        face_plus = 0.5 * (fluxes + shift_up(fluxes, up_flux, axis_dir)) - 0.5 * jnp.maximum(speeds, shift_up(speeds, up_speed, axis_dir)) * (above_cells - conserved)
        first_cells = first_slab(conserved, axis_dir)
        face_low = 0.5 * (low_flux + first_slab(fluxes, axis_dir)) - 0.5 * jnp.maximum(low_speed, first_slab(speeds, axis_dir)) * (first_cells - lower_ghost)
        net_flux = net_flux + face_plus - shift_down(face_plus, face_low, axis_dir)
        below_cells = shift_down(conserved, lower_ghost, axis_dir)
        vel_diffs.append(above_cells[1:4] / above_cells[0] - below_cells[1:4] / below_cells[0])
        speed_sum = speed_sum + speeds
    grad_sq = jnp.zeros_like(distance)
    for component in range(3):
        for axis_out in range(3):
            grad_entry = 0.5 * (normals[0, axis_out] * vel_diffs[0][component] + normals[1, axis_out] * vel_diffs[1][component] + normals[2, axis_out] * vel_diffs[2][component]) / volume
            grad_sq = grad_sq + grad_entry * grad_entry
    grad_norm = jnp.sqrt(grad_sq)
    nu_ratio = conserved[5] / conserved[0] / distance
    source = PROD_COEF * grad_norm * conserved[5] - DEST_COEF * conserved[0] * nu_ratio * nu_ratio
    rates = -net_flux / volume
    rates = jnp.concatenate([rates[:5], (rates[5] + source)[None]], axis=0)
    step_limit = COURANT * volume / jnp.max(speed_sum)
    return (rates, step_limit)

def all_rates(state, wall_dist, block_metric, links, inflow_cons):
    faces_i, faces_jk = jax.vmap(block_faces)(state)

    def block_rates(block_index):
        ghosts = []
        for face_index in range(6):
            face_link = links[block_index, face_index]
            if face_index < 2:
                partner_layer = faces_i[face_link[1], face_link[2]]
                own_layer = faces_i[block_index, face_index]
                oriented = make_ghost(partner_layer, own_layer, face_link[0], face_link[3], True)
            else:
                partner_layer = faces_jk[face_link[1], face_link[2] - 2]
                own_layer = faces_jk[block_index, face_index - 2]
                oriented = make_ghost(partner_layer, own_layer, face_link[0], face_link[3], False)
            ghosts.append(finish_ghost(oriented, own_layer, face_link[0], inflow_cons))
        return block_rate(state[block_index], ghosts, block_metric[block_index], wall_dist[block_index])
    return lax.map(block_rates, jnp.arange(BLK_ALL, dtype=jnp.int32))

def reference(state, wall_dist, block_metric, inflow, counts, links):
    inflow_cons = inflow_state(inflow)
    block_ids = jnp.arange(BLK_ALL, dtype=jnp.int32)
    in_use = block_ids % SLOTS < counts[block_ids // SLOTS]
    rates_first, limits = all_rates(state, wall_dist, block_metric, links, inflow_cons)
    time_step = jnp.min(jnp.where(in_use, limits, 1e+30))
    middle = state + time_step * rates_first
    rates_second, unused_limits = all_rates(middle, wall_dist, block_metric, links, inflow_cons)
    tendency = jnp.where(in_use[:, None, None, None], 0.5 * (rates_first + rates_second), 0.0)
    return (tendency, time_step)
```

```python
import jax
import jax.numpy as jnp
from jax import lax
from jax.experimental import pallas as pl
from jax.experimental.pallas import tpu as pltpu
from jax.sharding import PartitionSpec as P

NI = 16
NJ = 16
NK = 16
SLOTS = 3
FIELDS = 6
LANES = 128
OFFSETS = (-2, -1, 1, 2)
STRIDE = 8

GAMMA = 1.4
PROD_COEF = 0.1355
DEST_COEF = 3.239
COURANT = 0.5
WALL_SIGNS = (1.0, -1.0, -1.0, -1.0, 1.0, -1.0)

SEND = (8, 8, LANES)
LIMIT_ROW = 6
PLAN = 128
PLAN_I = 16
PLAN_FACE = 32

f32 = jnp.float32
i32 = jnp.int32


def iota(shape, axis):
    return lax.broadcasted_iota(i32, shape, axis)


def pick(values, index, axis):
    return jnp.take_along_axis(values, index, axis=axis, mode="promise_in_bounds")


def geometry(metric_ref, slot):
    normals = [
        [(1.0 if d == e else 0.0) + 0.25 * metric_ref[slot, 3 * d + e] for e in range(3)] for d in range(3)
    ]
    return normals, 1.0 + 0.25 * metric_ref[slot, 9]


def area_of(normal):
    total = normal[0] * normal[0] + normal[1] * normal[1] + normal[2] * normal[2]
    return jnp.sqrt(total)


def splat(value, shape):
    return jnp.full(shape, value, f32)


def primitives(cons):
    inverse = 1.0 / cons[0]
    velocity = [cons[1 + c] * inverse for c in range(3)]
    kinetic = cons[1] * velocity[0] + cons[2] * velocity[1] + cons[3] * velocity[2]
    pressure = (GAMMA - 1.0) * (cons[4] - 0.5 * kinetic)
    sound = jnp.sqrt(GAMMA * pressure * inverse)
    return inverse, velocity, pressure, sound


def fluxes_of(cons, prim, normal, area):
    _, velocity, pressure, sound = prim
    normal_vel = normal[0] * velocity[0] + normal[1] * velocity[1] + normal[2] * velocity[2]
    fluxes = [
        cons[0] * normal_vel,
        cons[1] * normal_vel + pressure * normal[0],
        cons[2] * normal_vel + pressure * normal[1],
        cons[3] * normal_vel + pressure * normal[2],
        (cons[4] + pressure) * normal_vel,
        cons[5] * normal_vel,
    ]
    return fluxes, jnp.abs(normal_vel) + sound * area


def edge(own, ghost, normal, area, sign):
    own_prim = primitives(own)
    ghost_prim = primitives(ghost)
    own_flux, own_speed = fluxes_of(own, own_prim, normal, area)
    ghost_flux, ghost_speed = fluxes_of(ghost, ghost_prim, normal, area)
    speed = sign * jnp.maximum(own_speed, ghost_speed)
    flux = [own_flux[f] + ghost_flux[f] - speed * (ghost[f] - own[f]) for f in range(FIELDS)]
    return flux, ghost_prim[1]


def split(values):
    return values[:, :LANES], values[:, LANES:]


def shifted_up(values, axis_dir):
    low, high = split(values)
    if axis_dir == 0:
        low, high = pltpu.roll(low, NI - 1, 0), pltpu.roll(high, NI - 1, 0)
    elif axis_dir == 1:
        low, high = pltpu.roll(low, LANES - NK, 1), pltpu.roll(high, LANES - NK, 1)
        low = jnp.where(iota(low.shape, 1) < LANES - NK, low, high)
    else:
        low, high = pltpu.roll(low, LANES - 1, 1), pltpu.roll(high, LANES - 1, 1)
    return jnp.concatenate([low, high], axis=1)


def shifted_down(values, axis_dir):
    low, high = split(values)
    if axis_dir == 0:
        low, high = pltpu.roll(low, 1, 0), pltpu.roll(high, 1, 0)
    elif axis_dir == 1:
        low, high = pltpu.roll(low, NK, 1), pltpu.roll(high, NK, 1)
        high = jnp.where(iota(high.shape, 1) < NK, low, high)
    else:
        low, high = pltpu.roll(low, 1, 1), pltpu.roll(high, 1, 1)
    return jnp.concatenate([low, high], axis=1)


def placed(compact, axis_dir):
    if axis_dir == 1:
        low = jnp.concatenate([compact, pltpu.roll(compact, 64, 1)], axis=0)
        high = jnp.concatenate([pltpu.roll(compact, 96, 1), pltpu.roll(compact, 32, 1)], axis=0)
        return low, high
    lane = iota((8, LANES), 1)
    index = lane // NK + jnp.where(lane % NK == NK - 1, 48, 32)
    rows = []
    for a in range(2):
        rows.append(jnp.concatenate([pick(compact, index + (64 * a + 8 * b), 1) for b in range(2)], axis=1))
    both = jnp.concatenate(rows, axis=0)
    return both, both


def put_high(values, high, axis_dir):
    if axis_dir == 0:
        return jnp.where(iota(values.shape, 0) == NI - 1, high, values)
    if axis_dir == 1:
        first, second = split(values)
        second = jnp.where(iota(second.shape, 1) >= LANES - NK, high, second)
        return jnp.concatenate([first, second], axis=1)
    return jnp.where(iota(values.shape, 1) % NK == NK - 1, high, values)


def put_low(values, low, axis_dir):
    if axis_dir == 0:
        return jnp.where(iota(values.shape, 0) == 0, low, values)
    if axis_dir == 1:
        first, second = split(values)
        first = jnp.where(iota(first.shape, 1) < NK, low, first)
        return jnp.concatenate([first, second], axis=1)
    return jnp.where(iota(values.shape, 1) % NK == 0, low, values)


def write_edges(values, slot, table_jk, table_i):
    lane = iota((8, LANES), 1)
    t = lane % NK
    group = lane // NK % 4
    index = jnp.where(
        group == 0,
        t,
        jnp.where(group == 1, LANES - NK + t, NK * (t % 8) + jnp.where(group == 3, NK - 1, 0)),
    )
    second = (group == 1) | ((group >= 2) & (t >= 8))
    for f in range(FIELDS):
        halves = []
        for a in range(2):
            rows = values[f][8 * a : 8 * a + 8]
            halves.append(jnp.where(second, pick(rows[:, LANES:], index, 1), pick(rows[:, :LANES], index, 1)))
        table_jk[slot, f] = jnp.where(lane < 64, halves[0], halves[1])
        for face in range(2):
            row = values[f][(NI - 1) * face : (NI - 1) * face + 1]
            at = 8 * (2 * slot + face) + f
            table_i[0, at : at + 1, :] = row[:, :LANES]
            table_i[1, at : at + 1, :] = row[:, LANES:]


def make_plan(links_ref, device, dev_count, plan_ref, mask_ref):
    def entry(slot, face):
        code, block, other = links_ref[slot, face, 0], links_ref[slot, face, 1], links_ref[slot, face, 2]
        partner_dev = lax.div(block, SLOTS)
        away = lax.rem(partner_dev - device + dev_count, dev_count)
        space = jnp.where(
            away == dev_count - 2, 0, jnp.where(away == dev_count - 1, 1, jnp.where(away == 1, 2, jnp.where(away == 2, 3, 4)))
        )
        space = jnp.where(code == 3, space, 4)
        return space, block - SLOTS * partner_dev, other

    for n in range(PLAN_I + 5):
        plan_ref[n] = 0
    for n in range(5):
        mask_ref[n] = 0
        mask_ref[8 + n] = 0
    entries = {}
    for slot in range(SLOTS):
        for face in range(6):
            space, partner_slot, other = entry(slot, face)
            if face < 2:
                plan_ref[PLAN_I + space] = 2 * slot + face
                plan_ref[PLAN_FACE + 2 * (6 * slot + face)] = jnp.where(
                    space < 4, 2 * SLOTS + space, 2 * partner_slot + (other & 1)
                )
                continue
            count = mask_ref[8 + space]
            mask_ref[8 + space] = count + 1
            plan_ref[3 * space + jnp.where(space < 4, jnp.minimum(count, 2), 0)] = 4 * slot + face - 2
            key = 4 * partner_slot + ((other - 2) & 3)
            mask_ref[space] = mask_ref[space] | lax.shift_left(jnp.int32(1), key)
            entries[slot, face] = (space, partner_slot, key)
    for (slot, face), (space, partner_slot, key) in entries.items():
        below = mask_ref[space] & (lax.shift_left(jnp.int32(1), key) - 1)
        below = below - (lax.shift_right_logical(below, 1) & 0x555)
        below = (below & 0x333) + (lax.shift_right_logical(below, 2) & 0x333)
        below = (below + lax.shift_right_logical(below, 4)) & 0xF0F
        rank = jnp.minimum((below + lax.shift_right_logical(below, 8)) & 0xF, 2)
        at = PLAN_FACE + 2 * (6 * slot + face)
        plan_ref[at] = jnp.where(space < 4, SLOTS + space, partner_slot)
        plan_ref[at + 1] = NK * jnp.where(space < 4, rank, key & 3)


def write_sends(table_jk, table_i, plan_ref, limit, send_refs):
    lane = iota((8, LANES), 1)
    group = lane // NK % 4
    base = (lane & 64) | (lane % NK)
    row = iota((8, LANES), 0)
    for n in range(len(OFFSETS)):
        chosen = []
        for q in range(3):
            source = plan_ref[3 * n + q]
            index = base + NK * (source & 3)
            slot = lax.shift_right_logical(source, 2)
            chosen.append([pick(table_jk[slot, f], index, 1) for f in range(FIELDS)])
        for f in range(FIELDS):
            send_refs[n][f] = jnp.where(group == 0, chosen[0][f], jnp.where(group == 1, chosen[1][f], chosen[2][f]))
        at = pl.multiple_of(8 * plan_ref[PLAN_I + n], 8)
        first = table_i[0, pl.ds(at, 8), :]
        second = table_i[1, pl.ds(at, 8), :]
        send_refs[n][6] = jnp.where(row == LIMIT_ROW, limit, jnp.where(row < FIELDS, first, 0.0))
        send_refs[n][7] = jnp.where(row < FIELDS, second, 0.0)


def jk_ghosts(slot, table_jk, links_ref, plan_ref, far):
    lane = iota((8, LANES), 1)
    row = iota((8, LANES), 0)
    t = lane % NK
    group = lane // NK % 4
    gathered = None
    code = jnp.zeros((8, LANES), i32)
    row_index = row
    for face in range(2, 6):
        at = PLAN_FACE + 2 * (6 * slot + face)
        source, start = plan_ref[at], plan_ref[at + 1]
        orient = links_ref[slot, face, 3]
        first_rev = lax.shift_right_logical(orient, 1) & 1
        second_rev = lax.shift_right_logical(orient, 2) & 1
        index = ((lane & 64) ^ (64 * first_rev)) + (t ^ (15 * second_rev)) + start
        here = group == face - 2
        code = jnp.where(here, links_ref[slot, face, 0], code)
        row_index = jnp.where(here, row ^ (7 * first_rev), row_index)
        layers = [pick(table_jk[source, f], index, 1) for f in range(FIELDS)]
        gathered = layers if gathered is None else [jnp.where(here, new, old) for new, old in zip(layers, gathered)]
    own = [table_jk[slot, f] for f in range(FIELDS)]
    ghosts = []
    joined, distant, wall = code == 3, code == 0, code == 1
    for f in range(FIELDS):
        mirrored = own[f] if WALL_SIGNS[f] > 0 else jnp.where(wall, -own[f], own[f])
        ghosts.append(jnp.where(joined, pick(gathered[f], row_index, 0), jnp.where(distant, far[f], mirrored)))
    return own, ghosts


def i_ghosts(table_i, ghost_i, links_ref, plan_ref, far):
    row = iota((8, 2 * LANES), 0)
    flat = iota((8, 2 * LANES), 1)
    code = jnp.zeros((8, 2 * LANES), i32)
    orient = jnp.zeros((8, 2 * LANES), i32)
    for n in range(2 * SLOTS):
        slot, face = n // 2, n % 2
        at = pl.multiple_of(8 * plan_ref[PLAN_FACE + 2 * (6 * slot + face)], 8)
        for b in range(2):
            ghost_i[b, 8 * n : 8 * n + 8, :] = table_i[b, pl.ds(at, 8), :]
        code = jnp.where(row == n, links_ref[slot, face, 0], code)
        orient = jnp.where(row == n, links_ref[slot, face, 3], orient)
    first = (flat // NK) ^ (15 * ((orient >> 1) & 1))
    second = (flat % NK) ^ (15 * ((orient >> 2) & 1))
    source = jnp.where((orient & 1) == 1, NK * second + first, NK * first + second)
    upper = source >= LANES
    index = source & (LANES - 1)
    joined, distant, wall = code == 3, code == 0, code == 1
    own, ghosts = [], []
    for f in range(FIELDS):
        mine = jnp.concatenate([table_i[b, pl.ds(f, 8, stride=8), :] for b in range(2)], axis=1)
        halves = [ghost_i[b, pl.ds(f, 8, stride=8), :] for b in range(2)]
        layer = []
        for b in range(2):
            at = slice(b * LANES, (b + 1) * LANES)
            layer.append(jnp.where(upper[:, at], pick(halves[1], index[:, at], 1), pick(halves[0], index[:, at], 1)))
        layer = jnp.concatenate(layer, axis=1)
        mirrored = mine if WALL_SIGNS[f] > 0 else jnp.where(wall, -mine, mine)
        own.append(mine)
        ghosts.append(jnp.where(joined, layer, jnp.where(distant, far[f], mirrored)))
    return own, ghosts


def far_field(inflow_ref):
    density, pressure = inflow_ref[0], inflow_ref[4]
    velocity = [inflow_ref[1 + c] for c in range(3)]
    squares = velocity[0] * velocity[0] + velocity[1] * velocity[1] + velocity[2] * velocity[2]
    energy = pressure * (1.0 / (GAMMA - 1.0)) + 0.5 * density * squares
    return [density] + [density * v for v in velocity] + [energy, density * inflow_ref[5]]


def section(load, distance_ref, links_ref, counts_ref, metric_ref, inflow_ref, plan_ref, table_jk, table_i, ghost_i, edge_i, store):
    far = far_field(inflow_ref)
    own, ghosts = i_ghosts(table_i, ghost_i, links_ref, plan_ref, far)
    row = iota((8, 2 * LANES), 0)
    normal = [None] * 3
    for e in range(3):
        value = splat((1.0 if e == 0 else 0.0) + 0.25 * metric_ref[0, e], row.shape)
        for slot in range(1, SLOTS):
            value = jnp.where(row // 2 == slot, (1.0 if e == 0 else 0.0) + 0.25 * metric_ref[slot, e], value)
        normal[e] = value
    sign = jnp.where(row % 2 == 1, 1.0, -1.0)
    flux, velocity = edge(own, ghosts, normal, area_of(normal), sign)
    for n, value in enumerate(flux + velocity):
        edge_i[n] = value

    group = iota((8, LANES), 1) // NK % 4
    sign_jk = jnp.where(group % 2 == 1, 1.0, -1.0)

    def one(slot):
        normals, volume = geometry(metric_ref, slot)
        own, ghosts = jk_ghosts(slot, table_jk, links_ref, plan_ref, far)
        lane_normal = [jnp.where(group < 2, normals[1][e], normals[2][e]) for e in range(3)]
        edge_flux, edge_velocity = edge(own, ghosts, lane_normal, area_of(lane_normal), sign_jk)
        cons = load(slot)
        prim = primitives(cons)
        inverse, velocity = prim[0], prim[1]
        half_inverse = splat(0.5, (1, 1)) / splat(volume, (1, 1))
        net = [None] * FIELDS
        differences = []
        for d in range(3):
            area = area_of([splat(normals[d][e], (1, 1)) for e in range(3)])
            fluxes, speed = fluxes_of(cons, prim, normals[d], area)
            speed = jnp.maximum(speed, shifted_up(speed, d))
            for f in range(FIELDS):
                if d == 0:
                    low = edge_i[f, 2 * slot : 2 * slot + 1, :]
                    high = edge_i[f, 2 * slot + 1 : 2 * slot + 2, :]
                else:
                    low, high = placed(edge_flux[f], d)
                above = fluxes[f] + shifted_up(fluxes[f], d) - speed * (shifted_up(cons[f], d) - cons[f])
                above = put_high(above, high, d)
                change = above - put_low(shifted_down(above, d), low, d)
                net[f] = change if net[f] is None else net[f] + change
            change = []
            for c in range(3):
                if d == 0:
                    low = edge_i[FIELDS + c, 2 * slot : 2 * slot + 1, :]
                    high = edge_i[FIELDS + c, 2 * slot + 1 : 2 * slot + 2, :]
                else:
                    low, high = placed(edge_velocity[c], d)
                change.append(put_high(shifted_up(velocity[c], d), high, d) - put_low(shifted_down(velocity[c], d), low, d))
            differences.append(change)
        squares = None
        for e in range(3):
            scaled = [splat(normals[d][e], (1, 1)) * half_inverse for d in range(3)]
            for c in range(3):
                entry = scaled[0] * differences[0][c] + scaled[1] * differences[1][c] + scaled[2] * differences[2][c]
                squares = entry * entry if squares is None else squares + entry * entry
        ratio = cons[5] * inverse / distance_ref[slot]
        source = PROD_COEF * jnp.sqrt(squares) * cons[5] - DEST_COEF * cons[0] * ratio * ratio
        rates = [-net[f] * half_inverse for f in range(FIELDS)]
        rates[5] = rates[5] + source
        store(slot, cons, rates)

    for slot in range(SLOTS):
        if slot == 0:
            one(slot)
        else:
            pl.when(slot < counts_ref[0])(lambda slot=slot: one(slot))


def first_kernel(dev_count, axis, links_ref, counts_ref, metric_ref, state_ref, *refs):
    send_refs, plan_ref = refs[:4], refs[4]
    table_jk, table_i, mask_ref = refs[5:]
    make_plan(links_ref, lax.axis_index(axis), dev_count, plan_ref, mask_ref)
    limit = None
    for slot in range(SLOTS):
        cons = [state_ref[slot, f] for f in range(FIELDS)]
        write_edges(cons, slot, table_jk, table_i)
        normals, volume = geometry(metric_ref, slot)
        _, velocity, _, sound = primitives(cons)
        total = None
        area = None
        for d in range(3):
            normal_vel = normals[d][0] * velocity[0] + normals[d][1] * velocity[1] + normals[d][2] * velocity[2]
            total = jnp.abs(normal_vel) if total is None else total + jnp.abs(normal_vel)
            one_area = area_of([splat(normals[d][e], (1, 1)) for e in range(3)])
            area = one_area if area is None else area + one_area
        total = total + sound * area
        own = COURANT * splat(volume, (1, 1)) / jnp.max(total, axis=(0, 1), keepdims=True)
        limit = own if limit is None else jnp.where(slot < counts_ref[0], jnp.minimum(limit, own), limit)
    write_sends(table_jk, table_i, plan_ref, jnp.broadcast_to(limit, (8, LANES)), send_refs)


def fill_tables(received, table_jk, table_i):
    for n in range(len(OFFSETS)):
        for f in range(FIELDS):
            table_jk[SLOTS + n, f] = received[n](f)
        for b in range(2):
            at = 8 * (2 * SLOTS + n)
            table_i[b, at : at + 8, :] = received[n](6 + b)


def second_kernel(links_ref, counts_ref, metric_ref, inflow_ref, plan_ref, state_ref, distance_ref, *refs):
    received, own_limit_ref = refs[:4], refs[4]
    rate_ref, send_refs = refs[5], refs[6:10]
    table_jk, table_i, ghost_i, edge_i = refs[10:]
    for slot in range(SLOTS):
        write_edges([state_ref[slot, f] for f in range(FIELDS)], slot, table_jk, table_i)
    fill_tables([lambda k, n=n: received[n][k] for n in range(4)], table_jk, table_i)
    limit = own_limit_ref[6, LIMIT_ROW : LIMIT_ROW + 1, :]
    for n in range(4):
        limit = jnp.minimum(limit, received[n][6, LIMIT_ROW : LIMIT_ROW + 1, :])

    def store(slot, cons, rates):
        for f in range(FIELDS):
            rate_ref[slot, f] = rates[f]

    section(
        lambda slot: [state_ref[slot, f] for f in range(FIELDS)],
        distance_ref, links_ref, counts_ref, metric_ref, inflow_ref, plan_ref, table_jk, table_i, ghost_i, edge_i, store,
    )
    for slot in range(SLOTS):
        def edges(slot=slot):
            write_edges([rate_ref[slot, f] for f in range(FIELDS)], slot, table_jk, table_i)
        if slot == 0:
            edges()
        else:
            pl.when(slot < counts_ref[0])(edges)
    write_sends(table_jk, table_i, plan_ref, jnp.broadcast_to(limit, (8, LANES)), send_refs)


def third_kernel(links_ref, counts_ref, metric_ref, inflow_ref, plan_ref, state_ref, distance_ref, rate_ref, *refs):
    first, second, limits_ref = refs[:4], refs[4:8], refs[8]
    tendency_ref, step_ref = refs[9:11]
    table_jk, table_i, ghost_i, edge_i, middle_ref = refs[11:]
    step = jnp.min(limits_ref[...], axis=(0, 1), keepdims=True)
    step_ref[...] = step
    fill_tables([lambda k, n=n: first[n][k] + step * second[n][k] for n in range(4)], table_jk, table_i)
    for slot in range(SLOTS):
        def edges(slot=slot):
            middle = [state_ref[slot, f] + step * rate_ref[slot, f] for f in range(FIELDS)]
            for f in range(FIELDS):
                middle_ref[slot, f] = middle[f]
            write_edges(middle, slot, table_jk, table_i)
        if slot == 0:
            edges()
        else:
            pl.when(slot < counts_ref[0])(edges)

    def store(slot, cons, rates):
        for f in range(FIELDS):
            tendency_ref[slot, f] = 0.5 * (rate_ref[slot, f] + rates[f])

    section(
        lambda slot: [middle_ref[slot, f] for f in range(FIELDS)],
        distance_ref, links_ref, counts_ref, metric_ref, inflow_ref, plan_ref, table_jk, table_i, ghost_i, edge_i, store,
    )
    for slot in range(1, SLOTS):
        @pl.when(slot >= counts_ref[0])
        def _(slot=slot):
            for f in range(FIELDS):
                tendency_ref[slot, f] = jnp.zeros((NI, NJ * NK), f32)


def in_smem():
    return pl.BlockSpec(memory_space=pltpu.SMEM)


def in_vmem():
    return pl.BlockSpec(memory_space=pltpu.VMEM)


TABLES = (
    pltpu.VMEM((SLOTS + 4, FIELDS, 8, LANES), f32),
    pltpu.VMEM((2, 8 * (2 * SLOTS + 4), LANES), f32),
)
SCRATCH = TABLES + (pltpu.VMEM((2, 64, LANES), f32), pltpu.VMEM((9, 8, 2 * LANES), f32))


def body(state, wall_dist, block_metric, inflow, counts, links):
    axis = "blk"
    dev_count = lax.axis_size(axis)
    send = jax.ShapeDtypeStruct(SEND, f32)
    block = jax.ShapeDtypeStruct(state.shape, f32)

    *sends, plan = pl.pallas_call(
        lambda *refs: first_kernel(dev_count, axis, *refs),
        out_shape=[send] * 4 + [jax.ShapeDtypeStruct((PLAN,), i32)],
        in_specs=[in_smem()] * 3 + [in_vmem()],
        out_specs=[in_vmem()] * 4 + [in_smem()],
        scratch_shapes=TABLES + (pltpu.SMEM((16,), i32),),
        name="faces",
    )(links, counts, block_metric, state)

    def exchanged(arrays):
        result = []
        for array, offset in zip(reversed(arrays), OFFSETS):
            pairs = [((p + offset) % dev_count, p) for p in range(dev_count)]
            result.append(lax.ppermute(array, axis, pairs))
        return result

    first = exchanged(sends)
    rate, *sends_two = pl.pallas_call(
        second_kernel,
        out_shape=[block] + [send] * 4,
        in_specs=[in_smem()] * 5 + [in_vmem()] * 7,
        out_specs=[in_vmem()] * 5,
        scratch_shapes=SCRATCH,
        name="rate_one",
    )(links, counts, block_metric, inflow, plan, state, wall_dist, *first, sends[0])

    second = exchanged(sends_two)
    nearby = sends_two[0][6, LIMIT_ROW]
    for array in second:
        nearby = jnp.minimum(nearby, array[6, LIMIT_ROW])
    members = dev_count // STRIDE
    groups = [[r + STRIDE * k for k in range(members)] for r in range(STRIDE)]
    limits = lax.all_to_all(
        jnp.broadcast_to(nearby, (members, LANES)), axis, 0, 0, axis_index_groups=groups, tiled=True
    )

    tendency, step = pl.pallas_call(
        third_kernel,
        out_shape=[block, jax.ShapeDtypeStruct((1, 1), f32)],
        in_specs=[in_smem()] * 5 + [in_vmem()] * 12,
        out_specs=[in_vmem()] * 2,
        scratch_shapes=SCRATCH + (pltpu.VMEM(state.shape, f32),),
        name="rate_two",
    )(links, counts, block_metric, inflow, plan, state, wall_dist, rate, *first, *second, limits)
    return tendency, step[0, 0]


def solution(mesh):
    return jax.shard_map(
        body,
        mesh=mesh,
        in_specs=(
            P("blk", None, None, None),
            P("blk", None, None),
            P("blk", None),
            P(),
            P("blk"),
            P("blk", None, None),
        ),
        out_specs=(P("blk", None, None, None), P()),
        check_vma=False,
    )
```

```python
import jax
import jax.numpy as jnp
from jax import lax
from jax.experimental import pallas as pl
from jax.experimental.pallas import tpu as pltpu
from jax.sharding import PartitionSpec as P

NI = 16
NJ = 16
NK = 16
SLOTS = 3
FIELDS = 6
LANES = 128
OFFSETS = (-2, -1, 1, 2)

GAMMA = 1.4
PROD_COEF = 0.1355
DEST_COEF = 3.239
COURANT = 0.5
WALL_SIGNS = (1.0, -1.0, -1.0, -1.0, 1.0, -1.0)

SEND = (8, 8, LANES)
PLAN = 128
PLAN_I = 16
PLAN_FACE = 32

f32 = jnp.float32
i32 = jnp.int32


def iota(shape, axis):
    return lax.broadcasted_iota(i32, shape, axis)


def pick(values, index, axis):
    return jnp.take_along_axis(values, index, axis=axis, mode="promise_in_bounds")


def geometry(metric_ref, slot):
    normals = [
        [(1.0 if d == e else 0.0) + 0.25 * metric_ref[slot, 3 * d + e] for e in range(3)] for d in range(3)
    ]
    return normals, 1.0 + 0.25 * metric_ref[slot, 9]


def area_of(normal):
    total = normal[0] * normal[0] + normal[1] * normal[1] + normal[2] * normal[2]
    return jnp.sqrt(total)


def splat(value, shape):
    return jnp.full(shape, value, f32)


def primitives(cons):
    inverse = 1.0 / cons[0]
    velocity = [cons[1 + c] * inverse for c in range(3)]
    kinetic = cons[1] * velocity[0] + cons[2] * velocity[1] + cons[3] * velocity[2]
    pressure = (GAMMA - 1.0) * (cons[4] - 0.5 * kinetic)
    sound = jnp.sqrt(GAMMA * pressure * inverse)
    return inverse, velocity, pressure, sound


def fluxes_of(cons, prim, normal, area):
    _, velocity, pressure, sound = prim
    normal_vel = normal[0] * velocity[0] + normal[1] * velocity[1] + normal[2] * velocity[2]
    fluxes = [
        cons[0] * normal_vel,
        cons[1] * normal_vel + pressure * normal[0],
        cons[2] * normal_vel + pressure * normal[1],
        cons[3] * normal_vel + pressure * normal[2],
        (cons[4] + pressure) * normal_vel,
        cons[5] * normal_vel,
    ]
    return fluxes, jnp.abs(normal_vel) + sound * area


def edge(own, ghost, normal, area, sign):
    own_prim = primitives(own)
    ghost_prim = primitives(ghost)
    own_flux, own_speed = fluxes_of(own, own_prim, normal, area)
    ghost_flux, ghost_speed = fluxes_of(ghost, ghost_prim, normal, area)
    speed = sign * jnp.maximum(own_speed, ghost_speed)
    flux = [own_flux[f] + ghost_flux[f] - speed * (ghost[f] - own[f]) for f in range(FIELDS)]
    return flux, ghost_prim[1]


def split(values):
    return values[:, :LANES], values[:, LANES:]


def shifted_up(values, axis_dir):
    low, high = split(values)
    if axis_dir == 0:
        low, high = pltpu.roll(low, NI - 1, 0), pltpu.roll(high, NI - 1, 0)
    elif axis_dir == 1:
        low, high = pltpu.roll(low, LANES - NK, 1), pltpu.roll(high, LANES - NK, 1)
        low = jnp.where(iota(low.shape, 1) < LANES - NK, low, high)
    else:
        low, high = pltpu.roll(low, LANES - 1, 1), pltpu.roll(high, LANES - 1, 1)
    return jnp.concatenate([low, high], axis=1)


def shifted_down(values, axis_dir):
    low, high = split(values)
    if axis_dir == 0:
        low, high = pltpu.roll(low, 1, 0), pltpu.roll(high, 1, 0)
    elif axis_dir == 1:
        low, high = pltpu.roll(low, NK, 1), pltpu.roll(high, NK, 1)
        high = jnp.where(iota(high.shape, 1) < NK, low, high)
    else:
        low, high = pltpu.roll(low, 1, 1), pltpu.roll(high, 1, 1)
    return jnp.concatenate([low, high], axis=1)


def placed(compact, axis_dir):
    if axis_dir == 1:
        low = jnp.concatenate([compact, pltpu.roll(compact, 64, 1)], axis=0)
        high = jnp.concatenate([pltpu.roll(compact, 96, 1), pltpu.roll(compact, 32, 1)], axis=0)
        return low, high
    lane = iota((8, LANES), 1)
    index = lane // NK + jnp.where(lane % NK == NK - 1, 48, 32)
    rows = []
    for a in range(2):
        rows.append(jnp.concatenate([pick(compact, index + (64 * a + 8 * b), 1) for b in range(2)], axis=1))
    both = jnp.concatenate(rows, axis=0)
    return both, both


def put_high(values, high, axis_dir):
    if axis_dir == 0:
        return jnp.where(iota(values.shape, 0) == NI - 1, high, values)
    if axis_dir == 1:
        first, second = split(values)
        second = jnp.where(iota(second.shape, 1) >= LANES - NK, high, second)
        return jnp.concatenate([first, second], axis=1)
    return jnp.where(iota(values.shape, 1) % NK == NK - 1, high, values)


def put_low(values, low, axis_dir):
    if axis_dir == 0:
        return jnp.where(iota(values.shape, 0) == 0, low, values)
    if axis_dir == 1:
        first, second = split(values)
        first = jnp.where(iota(first.shape, 1) < NK, low, first)
        return jnp.concatenate([first, second], axis=1)
    return jnp.where(iota(values.shape, 1) % NK == 0, low, values)


def write_edges(values, slot, table_jk, table_i):
    lane = iota((8, LANES), 1)
    t = lane % NK
    group = lane // NK % 4
    index = jnp.where(
        group == 0,
        t,
        jnp.where(group == 1, LANES - NK + t, NK * (t % 8) + jnp.where(group == 3, NK - 1, 0)),
    )
    second = (group == 1) | ((group >= 2) & (t >= 8))
    for f in range(FIELDS):
        halves = []
        for a in range(2):
            rows = values[f][8 * a : 8 * a + 8]
            halves.append(jnp.where(second, pick(rows[:, LANES:], index, 1), pick(rows[:, :LANES], index, 1)))
        table_jk[slot, f] = jnp.where(lane < 64, halves[0], halves[1])
        for face in range(2):
            row = values[f][(NI - 1) * face : (NI - 1) * face + 1]
            at = 8 * (2 * slot + face) + f
            table_i[0, at : at + 1, :] = row[:, :LANES]
            table_i[1, at : at + 1, :] = row[:, LANES:]


def make_plan(links_ref, device, dev_count, plan_ref, mask_ref):
    def entry(slot, face):
        code, block, other = links_ref[slot, 0, face], links_ref[slot, 1, face], links_ref[slot, 2, face]
        partner_dev = lax.div(block, SLOTS)
        away = lax.rem(partner_dev - device + dev_count, dev_count)
        space = jnp.where(
            away == dev_count - 2, 0, jnp.where(away == dev_count - 1, 1, jnp.where(away == 1, 2, jnp.where(away == 2, 3, 4)))
        )
        space = jnp.where(code == 3, space, 4)
        return space, block - SLOTS * partner_dev, other

    for n in range(PLAN_I + 5):
        plan_ref[n] = 0
    for n in range(5):
        mask_ref[n] = 0
        mask_ref[8 + n] = 0
    entries = {}
    for slot in range(SLOTS):
        for face in range(6):
            space, partner_slot, other = entry(slot, face)
            if face < 2:
                plan_ref[PLAN_I + space] = 2 * slot + face
                plan_ref[PLAN_FACE + 2 * (6 * slot + face)] = jnp.where(
                    space < 4, 2 * SLOTS + space, 2 * partner_slot + (other & 1)
                )
                continue
            count = mask_ref[8 + space]
            mask_ref[8 + space] = count + 1
            plan_ref[3 * space + jnp.where(space < 4, jnp.minimum(count, 2), 0)] = 4 * slot + face - 2
            key = 4 * partner_slot + ((other - 2) & 3)
            mask_ref[space] = mask_ref[space] | lax.shift_left(jnp.int32(1), key)
            entries[slot, face] = (space, partner_slot, key)
    for (slot, face), (space, partner_slot, key) in entries.items():
        below = mask_ref[space] & (lax.shift_left(jnp.int32(1), key) - 1)
        below = below - (lax.shift_right_logical(below, 1) & 0x555)
        below = (below & 0x333) + (lax.shift_right_logical(below, 2) & 0x333)
        below = (below + lax.shift_right_logical(below, 4)) & 0xF0F
        rank = jnp.minimum((below + lax.shift_right_logical(below, 8)) & 0xF, 2)
        at = PLAN_FACE + 2 * (6 * slot + face)
        plan_ref[at] = jnp.where(space < 4, SLOTS + space, partner_slot)
        plan_ref[at + 1] = NK * jnp.where(space < 4, rank, key & 3)


def write_sends(table_jk, table_i, plan_ref, send_refs):
    lane = iota((8, LANES), 1)
    group = lane // NK % 4
    base = (lane & 64) | (lane % NK)
    row = iota((8, LANES), 0)
    for n in range(len(OFFSETS)):
        chosen = []
        for q in range(3):
            source = plan_ref[3 * n + q]
            index = base + NK * (source & 3)
            slot = lax.shift_right_logical(source, 2)
            chosen.append([pick(table_jk[slot, f], index, 1) for f in range(FIELDS)])
        for f in range(FIELDS):
            send_refs[n][f] = jnp.where(group == 0, chosen[0][f], jnp.where(group == 1, chosen[1][f], chosen[2][f]))
        at = pl.multiple_of(8 * plan_ref[PLAN_I + n], 8)
        first = table_i[0, pl.ds(at, 8), :]
        second = table_i[1, pl.ds(at, 8), :]
        send_refs[n][6] = jnp.where(row < FIELDS, first, 0.0)
        send_refs[n][7] = jnp.where(row < FIELDS, second, 0.0)


def jk_ghosts(slot, table_jk, links_ref, plan_ref, far):
    lane = iota((8, LANES), 1)
    row = iota((8, LANES), 0)
    t = lane % NK
    group = lane // NK % 4
    gathered = None
    code = jnp.zeros((8, LANES), i32)
    row_index = row
    for face in range(2, 6):
        at = PLAN_FACE + 2 * (6 * slot + face)
        source, start = plan_ref[at], plan_ref[at + 1]
        orient = links_ref[slot, 3, face]
        first_rev = lax.shift_right_logical(orient, 1) & 1
        second_rev = lax.shift_right_logical(orient, 2) & 1
        index = ((lane & 64) ^ (64 * first_rev)) + (t ^ (15 * second_rev)) + start
        here = group == face - 2
        code = jnp.where(here, links_ref[slot, 0, face], code)
        row_index = jnp.where(here, row ^ (7 * first_rev), row_index)
        layers = [pick(table_jk[source, f], index, 1) for f in range(FIELDS)]
        gathered = layers if gathered is None else [jnp.where(here, new, old) for new, old in zip(layers, gathered)]
    own = [table_jk[slot, f] for f in range(FIELDS)]
    ghosts = []
    joined, distant, wall = code == 3, code == 0, code == 1
    for f in range(FIELDS):
        mirrored = own[f] if WALL_SIGNS[f] > 0 else jnp.where(wall, -own[f], own[f])
        ghosts.append(jnp.where(joined, pick(gathered[f], row_index, 0), jnp.where(distant, far[f], mirrored)))
    return own, ghosts


def i_ghosts(table_i, ghost_i, links_ref, plan_ref, far):
    row = iota((8, 2 * LANES), 0)
    flat = iota((8, 2 * LANES), 1)
    code = jnp.zeros((8, 2 * LANES), i32)
    orient = jnp.zeros((8, 2 * LANES), i32)
    for n in range(2 * SLOTS):
        slot, face = n // 2, n % 2
        at = pl.multiple_of(8 * plan_ref[PLAN_FACE + 2 * (6 * slot + face)], 8)
        for b in range(2):
            ghost_i[b, 8 * n : 8 * n + 8, :] = table_i[b, pl.ds(at, 8), :]
        code = jnp.where(row == n, links_ref[slot, 0, face], code)
        orient = jnp.where(row == n, links_ref[slot, 3, face], orient)
    first = (flat // NK) ^ (15 * ((orient >> 1) & 1))
    second = (flat % NK) ^ (15 * ((orient >> 2) & 1))
    source = jnp.where((orient & 1) == 1, NK * second + first, NK * first + second)
    upper = source >= LANES
    index = source & (LANES - 1)
    joined, distant, wall = code == 3, code == 0, code == 1
    own, ghosts = [], []
    for f in range(FIELDS):
        mine = jnp.concatenate([table_i[b, pl.ds(f, 8, stride=8), :] for b in range(2)], axis=1)
        halves = [ghost_i[b, pl.ds(f, 8, stride=8), :] for b in range(2)]
        layer = []
        for b in range(2):
            at = slice(b * LANES, (b + 1) * LANES)
            layer.append(jnp.where(upper[:, at], pick(halves[1], index[:, at], 1), pick(halves[0], index[:, at], 1)))
        layer = jnp.concatenate(layer, axis=1)
        mirrored = mine if WALL_SIGNS[f] > 0 else jnp.where(wall, -mine, mine)
        own.append(mine)
        ghosts.append(jnp.where(joined, layer, jnp.where(distant, far[f], mirrored)))
    return own, ghosts


def far_field(inflow_ref):
    density, pressure = inflow_ref[0], inflow_ref[4]
    velocity = [inflow_ref[1 + c] for c in range(3)]
    squares = velocity[0] * velocity[0] + velocity[1] * velocity[1] + velocity[2] * velocity[2]
    energy = pressure * (1.0 / (GAMMA - 1.0)) + 0.5 * density * squares
    return [density] + [density * v for v in velocity] + [energy, density * inflow_ref[5]]


def section(load, distance_ref, links_ref, counts_ref, metric_ref, inflow_ref, plan_ref, table_jk, table_i, ghost_i, edge_i, store):
    far = far_field(inflow_ref)
    own, ghosts = i_ghosts(table_i, ghost_i, links_ref, plan_ref, far)
    row = iota((8, 2 * LANES), 0)
    normal = [None] * 3
    for e in range(3):
        value = splat((1.0 if e == 0 else 0.0) + 0.25 * metric_ref[0, e], row.shape)
        for slot in range(1, SLOTS):
            value = jnp.where(row // 2 == slot, (1.0 if e == 0 else 0.0) + 0.25 * metric_ref[slot, e], value)
        normal[e] = value
    sign = jnp.where(row % 2 == 1, 1.0, -1.0)
    flux, velocity = edge(own, ghosts, normal, area_of(normal), sign)
    for n, value in enumerate(flux + velocity):
        edge_i[n] = value

    group = iota((8, LANES), 1) // NK % 4
    sign_jk = jnp.where(group % 2 == 1, 1.0, -1.0)

    def one(slot):
        normals, volume = geometry(metric_ref, slot)
        own, ghosts = jk_ghosts(slot, table_jk, links_ref, plan_ref, far)
        lane_normal = [jnp.where(group < 2, normals[1][e], normals[2][e]) for e in range(3)]
        edge_flux, edge_velocity = edge(own, ghosts, lane_normal, area_of(lane_normal), sign_jk)
        cons = load(slot)
        prim = primitives(cons)
        inverse, velocity = prim[0], prim[1]
        half_inverse = splat(0.5, (1, 1)) / splat(volume, (1, 1))
        net = [None] * FIELDS
        differences = []
        for d in range(3):
            area = area_of([splat(normals[d][e], (1, 1)) for e in range(3)])
            fluxes, speed = fluxes_of(cons, prim, normals[d], area)
            speed = jnp.maximum(speed, shifted_up(speed, d))
            for f in range(FIELDS):
                if d == 0:
                    low = edge_i[f, 2 * slot : 2 * slot + 1, :]
                    high = edge_i[f, 2 * slot + 1 : 2 * slot + 2, :]
                else:
                    low, high = placed(edge_flux[f], d)
                above = fluxes[f] + shifted_up(fluxes[f], d) - speed * (shifted_up(cons[f], d) - cons[f])
                above = put_high(above, high, d)
                change = above - put_low(shifted_down(above, d), low, d)
                net[f] = change if net[f] is None else net[f] + change
            change = []
            for c in range(3):
                if d == 0:
                    low = edge_i[FIELDS + c, 2 * slot : 2 * slot + 1, :]
                    high = edge_i[FIELDS + c, 2 * slot + 1 : 2 * slot + 2, :]
                else:
                    low, high = placed(edge_velocity[c], d)
                change.append(put_high(shifted_up(velocity[c], d), high, d) - put_low(shifted_down(velocity[c], d), low, d))
            differences.append(change)
        squares = None
        for e in range(3):
            scaled = [splat(normals[d][e], (1, 1)) * half_inverse for d in range(3)]
            for c in range(3):
                entry = scaled[0] * differences[0][c] + scaled[1] * differences[1][c] + scaled[2] * differences[2][c]
                squares = entry * entry if squares is None else squares + entry * entry
        ratio = cons[5] * inverse / distance_ref[slot]
        source = PROD_COEF * jnp.sqrt(squares) * cons[5] - DEST_COEF * cons[0] * ratio * ratio
        rates = [-net[f] * half_inverse for f in range(FIELDS)]
        rates[5] = rates[5] + source
        store(slot, cons, rates)

    for slot in range(SLOTS):
        if slot == 0:
            one(slot)
        else:
            pl.when(slot < counts_ref[0, 0])(lambda slot=slot: one(slot))


def first_kernel(dev_count, axis, links_ref, counts_ref, metric_ref, state_ref, *refs):
    send_refs, plan_ref, limits_ref = refs[:4], refs[4], refs[5]
    table_jk, table_i, mask_ref = refs[6:]
    make_plan(links_ref, lax.axis_index(axis), dev_count, plan_ref, mask_ref)
    limit = None
    for slot in range(SLOTS):
        cons = [state_ref[slot, f] for f in range(FIELDS)]
        write_edges(cons, slot, table_jk, table_i)
        normals, volume = geometry(metric_ref, slot)
        _, velocity, _, sound = primitives(cons)
        total = None
        area = None
        for d in range(3):
            normal_vel = normals[d][0] * velocity[0] + normals[d][1] * velocity[1] + normals[d][2] * velocity[2]
            total = jnp.abs(normal_vel) if total is None else total + jnp.abs(normal_vel)
            one_area = area_of([splat(normals[d][e], (1, 1)) for e in range(3)])
            area = one_area if area is None else area + one_area
        total = total + sound * area
        own = COURANT * splat(volume, (1, 1)) / jnp.max(total, axis=(0, 1), keepdims=True)
        limit = own if limit is None else jnp.where(slot < counts_ref[0, 0], jnp.minimum(limit, own), limit)
    limits_ref[...] = jnp.broadcast_to(limit, limits_ref.shape)
    write_sends(table_jk, table_i, plan_ref, send_refs)


def fill_tables(received, table_jk, table_i):
    for n in range(len(OFFSETS)):
        for f in range(FIELDS):
            table_jk[SLOTS + n, f] = received[n](f)
        for b in range(2):
            at = 8 * (2 * SLOTS + n)
            table_i[b, at : at + 8, :] = received[n](6 + b)


def second_kernel(links_ref, counts_ref, metric_ref, inflow_ref, plan_ref, state_ref, distance_ref, *refs):
    received = refs[:4]
    rate_ref, send_refs = refs[4], refs[5:9]
    table_jk, table_i, ghost_i, edge_i = refs[9:]
    for slot in range(SLOTS):
        write_edges([state_ref[slot, f] for f in range(FIELDS)], slot, table_jk, table_i)
    fill_tables([lambda k, n=n: received[n][k] for n in range(4)], table_jk, table_i)

    def store(slot, cons, rates):
        for f in range(FIELDS):
            rate_ref[slot, f] = rates[f]

    section(
        lambda slot: [state_ref[slot, f] for f in range(FIELDS)],
        distance_ref, links_ref, counts_ref, metric_ref, inflow_ref, plan_ref, table_jk, table_i, ghost_i, edge_i, store,
    )
    for slot in range(SLOTS):
        def edges(slot=slot):
            write_edges([rate_ref[slot, f] for f in range(FIELDS)], slot, table_jk, table_i)

        if slot == 0:
            edges()
        else:
            pl.when(slot < counts_ref[0, 0])(edges)
    write_sends(table_jk, table_i, plan_ref, send_refs)


def third_kernel(links_ref, counts_ref, metric_ref, inflow_ref, plan_ref, state_ref, distance_ref, rate_ref, *refs):
    first, second, limits_ref = refs[:4], refs[4:8], refs[8]
    tendency_ref, step_ref = refs[9:11]
    table_jk, table_i, ghost_i, edge_i, middle_ref = refs[11:]
    step = jnp.min(limits_ref[...], axis=(0, 1), keepdims=True)
    step_ref[...] = step
    fill_tables([lambda k, n=n: first[n][k] + step * second[n][k] for n in range(4)], table_jk, table_i)
    for slot in range(SLOTS):
        def edges(slot=slot):
            middle = [state_ref[slot, f] + step * rate_ref[slot, f] for f in range(FIELDS)]
            for f in range(FIELDS):
                middle_ref[slot, f] = middle[f]
            write_edges(middle, slot, table_jk, table_i)

        if slot == 0:
            edges()
        else:
            pl.when(slot < counts_ref[0, 0])(edges)

    def store(slot, cons, rates):
        for f in range(FIELDS):
            tendency_ref[slot, f] = 0.5 * (rate_ref[slot, f] + rates[f])

    section(
        lambda slot: [middle_ref[slot, f] for f in range(FIELDS)],
        distance_ref, links_ref, counts_ref, metric_ref, inflow_ref, plan_ref, table_jk, table_i, ghost_i, edge_i, store,
    )
    for slot in range(1, SLOTS):
        @pl.when(slot >= counts_ref[0, 0])
        def _(slot=slot):
            for f in range(FIELDS):
                tendency_ref[slot, f] = jnp.zeros((NI, NJ * NK), f32)


def in_smem():
    return pl.BlockSpec(memory_space=pltpu.SMEM)


def in_vmem():
    return pl.BlockSpec(memory_space=pltpu.VMEM)


TABLES = (
    pltpu.VMEM((SLOTS + 4, FIELDS, 8, LANES), f32),
    pltpu.VMEM((2, 8 * (2 * SLOTS + 4), LANES), f32),
)
SCRATCH = TABLES + (pltpu.VMEM((2, 64, LANES), f32), pltpu.VMEM((9, 8, 2 * LANES), f32))


def body(state, wall_dist, block_metric, inflow, counts, links):
    axis = "blk"
    dev_count = lax.axis_size(axis)
    links = jnp.transpose(links, (0, 2, 1))
    counts = counts.reshape(1, 1)
    send = pltpu.VMEM(SEND, f32)
    block = pltpu.VMEM(state.shape, f32)

    def near_core(array):
        return pltpu.with_memory_space_constraint(array, pltpu.VMEM)

    state, wall_dist = near_core(state), near_core(wall_dist)

    *sends, plan, limits = pl.pallas_call(
        lambda *refs: first_kernel(dev_count, axis, *refs),
        out_shape=[send] * 4 + [jax.ShapeDtypeStruct((PLAN,), i32), pltpu.VMEM((dev_count, LANES), f32)],
        in_specs=[in_smem()] * 3 + [in_vmem()],
        out_specs=[in_vmem()] * 4 + [in_smem(), in_vmem()],
        scratch_shapes=TABLES + (pltpu.SMEM((16,), i32),),
        name="faces",
    )(links, counts, block_metric, state)

    def exchanged(arrays):
        result = []
        for array, offset in zip(reversed(arrays), OFFSETS):
            pairs = [((p + offset) % dev_count, p) for p in range(dev_count)]
            result.append(lax.ppermute(array, axis, pairs))
        return result

    limits = lax.all_to_all(limits, axis, 0, 0, tiled=True)
    first = exchanged(sends)
    rate, *sends_two = pl.pallas_call(
        second_kernel,
        out_shape=[block] + [send] * 4,
        in_specs=[in_smem()] * 5 + [in_vmem()] * 6,
        out_specs=[in_vmem()] * 5,
        scratch_shapes=SCRATCH,
        name="rate_one",
    )(links, counts, block_metric, inflow, plan, state, wall_dist, *map(near_core, first))

    second = exchanged(sends_two)

    tendency, step = pl.pallas_call(
        third_kernel,
        out_shape=[jax.ShapeDtypeStruct(state.shape, f32), jax.ShapeDtypeStruct((1, 1), f32)],
        in_specs=[in_smem()] * 5 + [in_vmem()] * 12,
        out_specs=[in_vmem()] * 2,
        scratch_shapes=SCRATCH + (pltpu.VMEM(state.shape, f32),),
        name="rate_two",
    )(links, counts, block_metric, inflow, plan, state, wall_dist, near_core(rate), *map(near_core, first), *map(near_core, second), near_core(limits))
    return tendency, step[0, 0]


def solution(mesh):
    return jax.shard_map(
        body,
        mesh=mesh,
        in_specs=(
            P("blk", None, None, None),
            P("blk", None, None),
            P("blk", None),
            P(),
            P("blk"),
            P("blk", None, None),
        ),
        out_specs=(P("blk", None, None, None), P()),
        check_vma=False,
    )
```

```python
import jax
import jax.numpy as jnp
from jax import lax
from jax.experimental import pallas as pl
from jax.experimental.pallas import tpu as pltpu
from jax.sharding import PartitionSpec as P

NI = 16
NJ = 16
NK = 16
SLOTS = 3
FIELDS = 6
LANES = 128
OFFSETS = (-2, -1, 1, 2)

GAMMA = 1.4
PROD_COEF = 0.1355
DEST_COEF = 3.239
COURANT = 0.5
WALL_SIGNS = (1.0, -1.0, -1.0, -1.0, 1.0, -1.0)

SEND = (8, 8, LANES)
PLAN = 128
PLAN_I = 16
PLAN_FACE = 32

f32 = jnp.float32
i32 = jnp.int32


def iota(shape, axis):
    return lax.broadcasted_iota(i32, shape, axis)


def pick(values, index, axis):
    return jnp.take_along_axis(values, index, axis=axis, mode="promise_in_bounds")


def geometry(metric_ref, slot):
    normals = [
        [(1.0 if d == e else 0.0) + 0.25 * metric_ref[slot, 3 * d + e] for e in range(3)] for d in range(3)
    ]
    return normals, 1.0 + 0.25 * metric_ref[slot, 9]


def area_of(normal):
    total = normal[0] * normal[0] + normal[1] * normal[1] + normal[2] * normal[2]
    return jnp.sqrt(total)


def splat(value, shape):
    return jnp.full(shape, value, f32)


def primitives(cons):
    inverse = 1.0 / cons[0]
    velocity = [cons[1 + c] * inverse for c in range(3)]
    kinetic = cons[1] * velocity[0] + cons[2] * velocity[1] + cons[3] * velocity[2]
    pressure = (GAMMA - 1.0) * (cons[4] - 0.5 * kinetic)
    sound = jnp.sqrt(GAMMA * pressure * inverse)
    return inverse, velocity, pressure, sound


def fluxes_of(cons, prim, normal, area):
    _, velocity, pressure, sound = prim
    normal_vel = normal[0] * velocity[0] + normal[1] * velocity[1] + normal[2] * velocity[2]
    fluxes = [
        cons[0] * normal_vel,
        cons[1] * normal_vel + pressure * normal[0],
        cons[2] * normal_vel + pressure * normal[1],
        cons[3] * normal_vel + pressure * normal[2],
        (cons[4] + pressure) * normal_vel,
        cons[5] * normal_vel,
    ]
    return fluxes, jnp.abs(normal_vel) + sound * area


def edge(own, ghost, normal, area, sign):
    own_prim = primitives(own)
    ghost_prim = primitives(ghost)
    own_flux, own_speed = fluxes_of(own, own_prim, normal, area)
    ghost_flux, ghost_speed = fluxes_of(ghost, ghost_prim, normal, area)
    speed = sign * jnp.maximum(own_speed, ghost_speed)
    flux = [own_flux[f] + ghost_flux[f] - speed * (ghost[f] - own[f]) for f in range(FIELDS)]
    return flux, ghost_prim[1]


def split(values):
    return values[:, :LANES], values[:, LANES:]


def shifted_up(values, axis_dir):
    low, high = split(values)
    if axis_dir == 0:
        low, high = pltpu.roll(low, NI - 1, 0), pltpu.roll(high, NI - 1, 0)
    elif axis_dir == 1:
        low, high = pltpu.roll(low, LANES - NK, 1), pltpu.roll(high, LANES - NK, 1)
        low = jnp.where(iota(low.shape, 1) < LANES - NK, low, high)
    else:
        low, high = pltpu.roll(low, LANES - 1, 1), pltpu.roll(high, LANES - 1, 1)
    return jnp.concatenate([low, high], axis=1)


def shifted_down(values, axis_dir):
    low, high = split(values)
    if axis_dir == 0:
        low, high = pltpu.roll(low, 1, 0), pltpu.roll(high, 1, 0)
    elif axis_dir == 1:
        low, high = pltpu.roll(low, NK, 1), pltpu.roll(high, NK, 1)
        high = jnp.where(iota(high.shape, 1) < NK, low, high)
    else:
        low, high = pltpu.roll(low, 1, 1), pltpu.roll(high, 1, 1)
    return jnp.concatenate([low, high], axis=1)


def placed(compact, axis_dir):
    if axis_dir == 1:
        low = jnp.concatenate([compact, pltpu.roll(compact, 64, 1)], axis=0)
        high = jnp.concatenate([pltpu.roll(compact, 96, 1), pltpu.roll(compact, 32, 1)], axis=0)
        return low, high
    lane = iota((8, LANES), 1)
    index = lane // NK + jnp.where(lane % NK == NK - 1, 48, 32)
    rows = []
    for a in range(2):
        rows.append(jnp.concatenate([pick(compact, index + (64 * a + 8 * b), 1) for b in range(2)], axis=1))
    both = jnp.concatenate(rows, axis=0)
    return both, both


def put_high(values, high, axis_dir):
    if axis_dir == 0:
        return jnp.where(iota(values.shape, 0) == NI - 1, high, values)
    if axis_dir == 1:
        first, second = split(values)
        second = jnp.where(iota(second.shape, 1) >= LANES - NK, high, second)
        return jnp.concatenate([first, second], axis=1)
    return jnp.where(iota(values.shape, 1) % NK == NK - 1, high, values)


def put_low(values, low, axis_dir):
    if axis_dir == 0:
        return jnp.where(iota(values.shape, 0) == 0, low, values)
    if axis_dir == 1:
        first, second = split(values)
        first = jnp.where(iota(first.shape, 1) < NK, low, first)
        return jnp.concatenate([first, second], axis=1)
    return jnp.where(iota(values.shape, 1) % NK == 0, low, values)


def write_edges(values, slot, table_jk, table_i):
    lane = iota((8, LANES), 1)
    t = lane % NK
    group = lane // NK % 4
    index = jnp.where(
        group == 0,
        t,
        jnp.where(group == 1, LANES - NK + t, NK * (t % 8) + jnp.where(group == 3, NK - 1, 0)),
    )
    second = (group == 1) | ((group >= 2) & (t >= 8))
    for f in range(FIELDS):
        halves = []
        for a in range(2):
            rows = values[f][8 * a : 8 * a + 8]
            halves.append(jnp.where(second, pick(rows[:, LANES:], index, 1), pick(rows[:, :LANES], index, 1)))
        table_jk[slot, f] = jnp.where(lane < 64, halves[0], halves[1])
        for face in range(2):
            row = values[f][(NI - 1) * face : (NI - 1) * face + 1]
            at = 8 * (2 * slot + face) + f
            table_i[0, at : at + 1, :] = row[:, :LANES]
            table_i[1, at : at + 1, :] = row[:, LANES:]


def make_plan(links_ref, device, dev_count, plan_ref, mask_ref):
    def entry(slot, face):
        code, block, other = links_ref[slot, 0, face], links_ref[slot, 1, face], links_ref[slot, 2, face]
        partner_dev = lax.div(block, SLOTS)
        away = lax.rem(partner_dev - device + dev_count, dev_count)
        space = jnp.where(
            away == dev_count - 2, 0, jnp.where(away == dev_count - 1, 1, jnp.where(away == 1, 2, jnp.where(away == 2, 3, 4)))
        )
        space = jnp.where(code == 3, space, 4)
        return space, block - SLOTS * partner_dev, other

    for n in range(PLAN_I + 5):
        plan_ref[n] = 0
    for n in range(5):
        mask_ref[n] = 0
        mask_ref[8 + n] = 0
    entries = {}
    for slot in range(SLOTS):
        for face in range(6):
            space, partner_slot, other = entry(slot, face)
            if face < 2:
                plan_ref[PLAN_I + space] = 2 * slot + face
                plan_ref[PLAN_FACE + 2 * (6 * slot + face)] = jnp.where(
                    space < 4, 2 * SLOTS + space, 2 * partner_slot + (other & 1)
                )
                continue
            count = mask_ref[8 + space]
            mask_ref[8 + space] = count + 1
            plan_ref[3 * space + jnp.where(space < 4, jnp.minimum(count, 2), 0)] = 4 * slot + face - 2
            key = 4 * partner_slot + ((other - 2) & 3)
            mask_ref[space] = mask_ref[space] | lax.shift_left(jnp.int32(1), key)
            entries[slot, face] = (space, partner_slot, key)
    for (slot, face), (space, partner_slot, key) in entries.items():
        below = mask_ref[space] & (lax.shift_left(jnp.int32(1), key) - 1)
        below = below - (lax.shift_right_logical(below, 1) & 0x555)
        below = (below & 0x333) + (lax.shift_right_logical(below, 2) & 0x333)
        below = (below + lax.shift_right_logical(below, 4)) & 0xF0F
        rank = jnp.minimum((below + lax.shift_right_logical(below, 8)) & 0xF, 2)
        at = PLAN_FACE + 2 * (6 * slot + face)
        plan_ref[at] = jnp.where(space < 4, SLOTS + space, partner_slot)
        plan_ref[at + 1] = NK * jnp.where(space < 4, rank, key & 3)


def write_sends(table_jk, table_i, plan_ref, send_refs):
    lane = iota((8, LANES), 1)
    group = lane // NK % 4
    base = (lane & 64) | (lane % NK)
    row = iota((8, LANES), 0)
    for n in range(len(OFFSETS)):
        chosen = []
        for q in range(3):
            source = plan_ref[3 * n + q]
            index = base + NK * (source & 3)
            slot = lax.shift_right_logical(source, 2)
            chosen.append([pick(table_jk[slot, f], index, 1) for f in range(FIELDS)])
        for f in range(FIELDS):
            send_refs[n][f] = jnp.where(group == 0, chosen[0][f], jnp.where(group == 1, chosen[1][f], chosen[2][f]))
        at = pl.multiple_of(8 * plan_ref[PLAN_I + n], 8)
        first = table_i[0, pl.ds(at, 8), :]
        second = table_i[1, pl.ds(at, 8), :]
        send_refs[n][6] = jnp.where(row < FIELDS, first, 0.0)
        send_refs[n][7] = jnp.where(row < FIELDS, second, 0.0)


def jk_ghosts(slot, table_jk, links_ref, plan_ref, far):
    lane = iota((8, LANES), 1)
    row = iota((8, LANES), 0)
    t = lane % NK
    group = lane // NK % 4
    gathered = None
    code = jnp.zeros((8, LANES), i32)
    row_index = row
    for face in range(2, 6):
        at = PLAN_FACE + 2 * (6 * slot + face)
        source, start = plan_ref[at], plan_ref[at + 1]
        orient = links_ref[slot, 3, face]
        first_rev = lax.shift_right_logical(orient, 1) & 1
        second_rev = lax.shift_right_logical(orient, 2) & 1
        index = ((lane & 64) ^ (64 * first_rev)) + (t ^ (15 * second_rev)) + start
        here = group == face - 2
        code = jnp.where(here, links_ref[slot, 0, face], code)
        row_index = jnp.where(here, row ^ (7 * first_rev), row_index)
        layers = [pick(table_jk[source, f], index, 1) for f in range(FIELDS)]
        gathered = layers if gathered is None else [jnp.where(here, new, old) for new, old in zip(layers, gathered)]
    own = [table_jk[slot, f] for f in range(FIELDS)]
    ghosts = []
    joined, distant, wall = code == 3, code == 0, code == 1
    for f in range(FIELDS):
        mirrored = own[f] if WALL_SIGNS[f] > 0 else jnp.where(wall, -own[f], own[f])
        ghosts.append(jnp.where(joined, pick(gathered[f], row_index, 0), jnp.where(distant, far[f], mirrored)))
    return own, ghosts


def i_ghosts(table_i, ghost_i, links_ref, plan_ref, far):
    row = iota((8, 2 * LANES), 0)
    flat = iota((8, 2 * LANES), 1)
    code = jnp.zeros((8, 2 * LANES), i32)
    orient = jnp.zeros((8, 2 * LANES), i32)
    for n in range(2 * SLOTS):
        slot, face = n // 2, n % 2
        at = pl.multiple_of(8 * plan_ref[PLAN_FACE + 2 * (6 * slot + face)], 8)
        for b in range(2):
            ghost_i[b, 8 * n : 8 * n + 8, :] = table_i[b, pl.ds(at, 8), :]
        code = jnp.where(row == n, links_ref[slot, 0, face], code)
        orient = jnp.where(row == n, links_ref[slot, 3, face], orient)
    first = (flat // NK) ^ (15 * ((orient >> 1) & 1))
    second = (flat % NK) ^ (15 * ((orient >> 2) & 1))
    source = jnp.where((orient & 1) == 1, NK * second + first, NK * first + second)
    upper = source >= LANES
    index = source & (LANES - 1)
    joined, distant, wall = code == 3, code == 0, code == 1
    own, ghosts = [], []
    for f in range(FIELDS):
        mine = jnp.concatenate([table_i[b, pl.ds(f, 8, stride=8), :] for b in range(2)], axis=1)
        halves = [ghost_i[b, pl.ds(f, 8, stride=8), :] for b in range(2)]
        layer = []
        for b in range(2):
            at = slice(b * LANES, (b + 1) * LANES)
            layer.append(jnp.where(upper[:, at], pick(halves[1], index[:, at], 1), pick(halves[0], index[:, at], 1)))
        layer = jnp.concatenate(layer, axis=1)
        mirrored = mine if WALL_SIGNS[f] > 0 else jnp.where(wall, -mine, mine)
        own.append(mine)
        ghosts.append(jnp.where(joined, layer, jnp.where(distant, far[f], mirrored)))
    return own, ghosts


def far_field(inflow_ref):
    density, pressure = inflow_ref[0], inflow_ref[4]
    velocity = [inflow_ref[1 + c] for c in range(3)]
    squares = velocity[0] * velocity[0] + velocity[1] * velocity[1] + velocity[2] * velocity[2]
    energy = pressure * (1.0 / (GAMMA - 1.0)) + 0.5 * density * squares
    return [density] + [density * v for v in velocity] + [energy, density * inflow_ref[5]]


def section(load, distance_ref, links_ref, counts_ref, metric_ref, inflow_ref, plan_ref, table_jk, table_i, ghost_i, edge_i, store):
    far = far_field(inflow_ref)
    own, ghosts = i_ghosts(table_i, ghost_i, links_ref, plan_ref, far)
    row = iota((8, 2 * LANES), 0)
    normal = [None] * 3
    for e in range(3):
        value = splat((1.0 if e == 0 else 0.0) + 0.25 * metric_ref[0, e], row.shape)
        for slot in range(1, SLOTS):
            value = jnp.where(row // 2 == slot, (1.0 if e == 0 else 0.0) + 0.25 * metric_ref[slot, e], value)
        normal[e] = value
    sign = jnp.where(row % 2 == 1, 1.0, -1.0)
    flux, velocity = edge(own, ghosts, normal, area_of(normal), sign)
    for n, value in enumerate(flux + velocity):
        edge_i[n] = value

    group = iota((8, LANES), 1) // NK % 4
    sign_jk = jnp.where(group % 2 == 1, 1.0, -1.0)

    def one(slot):
        normals, volume = geometry(metric_ref, slot)
        own, ghosts = jk_ghosts(slot, table_jk, links_ref, plan_ref, far)
        lane_normal = [jnp.where(group < 2, normals[1][e], normals[2][e]) for e in range(3)]
        edge_flux, edge_velocity = edge(own, ghosts, lane_normal, area_of(lane_normal), sign_jk)
        cons = load(slot)
        prim = primitives(cons)
        inverse, velocity = prim[0], prim[1]
        half_inverse = splat(0.5, (1, 1)) / splat(volume, (1, 1))
        net = [None] * FIELDS
        differences = []
        for d in range(3):
            area = area_of([splat(normals[d][e], (1, 1)) for e in range(3)])
            fluxes, speed = fluxes_of(cons, prim, normals[d], area)
            speed = jnp.maximum(speed, shifted_up(speed, d))
            for f in range(FIELDS):
                if d == 0:
                    low = edge_i[f, 2 * slot : 2 * slot + 1, :]
                    high = edge_i[f, 2 * slot + 1 : 2 * slot + 2, :]
                else:
                    low, high = placed(edge_flux[f], d)
                above = fluxes[f] + shifted_up(fluxes[f], d) - speed * (shifted_up(cons[f], d) - cons[f])
                above = put_high(above, high, d)
                change = above - put_low(shifted_down(above, d), low, d)
                net[f] = change if net[f] is None else net[f] + change
            change = []
            for c in range(3):
                if d == 0:
                    low = edge_i[FIELDS + c, 2 * slot : 2 * slot + 1, :]
                    high = edge_i[FIELDS + c, 2 * slot + 1 : 2 * slot + 2, :]
                else:
                    low, high = placed(edge_velocity[c], d)
                change.append(put_high(shifted_up(velocity[c], d), high, d) - put_low(shifted_down(velocity[c], d), low, d))
            differences.append(change)
        squares = None
        for e in range(3):
            scaled = [splat(normals[d][e], (1, 1)) * half_inverse for d in range(3)]
            for c in range(3):
                entry = scaled[0] * differences[0][c] + scaled[1] * differences[1][c] + scaled[2] * differences[2][c]
                squares = entry * entry if squares is None else squares + entry * entry
        ratio = cons[5] * inverse / distance_ref[slot]
        source = PROD_COEF * jnp.sqrt(squares) * cons[5] - DEST_COEF * cons[0] * ratio * ratio
        rates = [-net[f] * half_inverse for f in range(FIELDS)]
        rates[5] = rates[5] + source
        store(slot, cons, rates)

    for slot in range(SLOTS):
        if slot == 0:
            one(slot)
        else:
            pl.when(slot < counts_ref[0, 0])(lambda slot=slot: one(slot))


def first_kernel(dev_count, axis, links_ref, counts_ref, metric_ref, state_ref, *refs):
    send_refs, plan_ref, limits_ref = refs[:4], refs[4], refs[5]
    table_jk, table_i, mask_ref = refs[6:]
    make_plan(links_ref, lax.axis_index(axis), dev_count, plan_ref, mask_ref)
    limit = None
    for slot in range(SLOTS):
        cons = [state_ref[slot, f] for f in range(FIELDS)]
        write_edges(cons, slot, table_jk, table_i)
        normals, volume = geometry(metric_ref, slot)
        _, velocity, _, sound = primitives(cons)
        total = None
        area = None
        for d in range(3):
            normal_vel = normals[d][0] * velocity[0] + normals[d][1] * velocity[1] + normals[d][2] * velocity[2]
            total = jnp.abs(normal_vel) if total is None else total + jnp.abs(normal_vel)
            one_area = area_of([splat(normals[d][e], (1, 1)) for e in range(3)])
            area = one_area if area is None else area + one_area
        total = total + sound * area
        own = COURANT * splat(volume, (1, 1)) / jnp.max(total, axis=(0, 1), keepdims=True)
        limit = own if limit is None else jnp.where(slot < counts_ref[0, 0], jnp.minimum(limit, own), limit)
    limits_ref[...] = jnp.broadcast_to(limit, limits_ref.shape)
    write_sends(table_jk, table_i, plan_ref, send_refs)


def fill_tables(received, table_jk, table_i):
    for n in range(len(OFFSETS)):
        for f in range(FIELDS):
            table_jk[SLOTS + n, f] = received[n](f)
        for b in range(2):
            at = 8 * (2 * SLOTS + n)
            table_i[b, at : at + 8, :] = received[n](6 + b)


def second_kernel(links_ref, counts_ref, metric_ref, inflow_ref, plan_ref, state_ref, distance_ref, *refs):
    received = refs[:4]
    rate_ref, send_refs = refs[4], refs[5:9]
    table_jk, table_i, ghost_i, edge_i = refs[9:]
    for slot in range(SLOTS):
        write_edges([state_ref[slot, f] for f in range(FIELDS)], slot, table_jk, table_i)
    fill_tables([lambda k, n=n: received[n][k] for n in range(4)], table_jk, table_i)

    def store(slot, cons, rates):
        for f in range(FIELDS):
            rate_ref[slot, f] = rates[f]

    section(
        lambda slot: [state_ref[slot, f] for f in range(FIELDS)],
        distance_ref, links_ref, counts_ref, metric_ref, inflow_ref, plan_ref, table_jk, table_i, ghost_i, edge_i, store,
    )
    for slot in range(SLOTS):
        def edges(slot=slot):
            write_edges([rate_ref[slot, f] for f in range(FIELDS)], slot, table_jk, table_i)

        if slot == 0:
            edges()
        else:
            pl.when(slot < counts_ref[0, 0])(edges)
    write_sends(table_jk, table_i, plan_ref, send_refs)


def third_kernel(links_ref, counts_ref, metric_ref, inflow_ref, plan_ref, state_ref, distance_ref, rate_ref, *refs):
    first, second, limits_ref = refs[:4], refs[4:8], refs[8]
    tendency_ref, step_ref = refs[9:11]
    table_jk, table_i, ghost_i, edge_i, middle_ref = refs[11:]
    step = jnp.min(limits_ref[...], axis=(0, 1), keepdims=True)
    step_ref[...] = step
    fill_tables([lambda k, n=n: first[n][k] + step * second[n][k] for n in range(4)], table_jk, table_i)
    for slot in range(SLOTS):
        def edges(slot=slot):
            middle = [state_ref[slot, f] + step * rate_ref[slot, f] for f in range(FIELDS)]
            for f in range(FIELDS):
                middle_ref[slot, f] = middle[f]
            write_edges(middle, slot, table_jk, table_i)

        if slot == 0:
            edges()
        else:
            pl.when(slot < counts_ref[0, 0])(edges)

    def store(slot, cons, rates):
        for f in range(FIELDS):
            tendency_ref[slot, f] = 0.5 * (rate_ref[slot, f] + rates[f])

    section(
        lambda slot: [middle_ref[slot, f] for f in range(FIELDS)],
        distance_ref, links_ref, counts_ref, metric_ref, inflow_ref, plan_ref, table_jk, table_i, ghost_i, edge_i, store,
    )
    for slot in range(1, SLOTS):
        @pl.when(slot >= counts_ref[0, 0])
        def _(slot=slot):
            for f in range(FIELDS):
                tendency_ref[slot, f] = jnp.zeros((NI, NJ * NK), f32)


def in_smem():
    return pl.BlockSpec(memory_space=pltpu.SMEM)


def in_vmem():
    return pl.BlockSpec(memory_space=pltpu.VMEM)


TABLES = (
    pltpu.VMEM((SLOTS + 4, FIELDS, 8, LANES), f32),
    pltpu.VMEM((2, 8 * (2 * SLOTS + 4), LANES), f32),
)
SCRATCH = TABLES + (pltpu.VMEM((2, 64, LANES), f32), pltpu.VMEM((9, 8, 2 * LANES), f32))


def body(state, wall_dist, block_metric, inflow, counts, links):
    axis = "blk"
    dev_count = lax.axis_size(axis)
    links = jnp.transpose(links, (0, 2, 1))
    counts = counts.reshape(1, 1)
    send = pltpu.VMEM(SEND, f32)
    block = pltpu.VMEM(state.shape, f32)

    def near_core(array):
        return pltpu.with_memory_space_constraint(array, pltpu.VMEM)

    state_near, wall_dist = near_core(state), near_core(wall_dist)

    *sends, plan, limits = pl.pallas_call(
        lambda *refs: first_kernel(dev_count, axis, *refs),
        out_shape=[send] * 4 + [jax.ShapeDtypeStruct((PLAN,), i32), pltpu.VMEM((dev_count, LANES), f32)],
        in_specs=[in_smem()] * 3 + [in_vmem()],
        out_specs=[in_vmem()] * 4 + [in_smem(), in_vmem()],
        scratch_shapes=TABLES + (pltpu.SMEM((16,), i32),),
        name="faces",
    )(links, counts, block_metric, state)

    def exchanged(arrays):
        result = []
        for array, offset in zip(reversed(arrays), OFFSETS):
            pairs = [((p + offset) % dev_count, p) for p in range(dev_count)]
            result.append(lax.ppermute(array, axis, pairs))
        return result

    limits = lax.all_to_all(limits, axis, 0, 0, tiled=True)
    first = exchanged(sends)
    rate, *sends_two = pl.pallas_call(
        second_kernel,
        out_shape=[block] + [send] * 4,
        in_specs=[in_smem()] * 5 + [in_vmem()] * 6,
        out_specs=[in_vmem()] * 5,
        scratch_shapes=SCRATCH,
        name="rate_one",
    )(links, counts, block_metric, inflow, plan, state_near, wall_dist, *map(near_core, first))

    second = exchanged(sends_two)

    tendency, step = pl.pallas_call(
        third_kernel,
        out_shape=[jax.ShapeDtypeStruct(state.shape, f32), jax.ShapeDtypeStruct((1, 1), f32)],
        in_specs=[in_smem()] * 5 + [in_vmem()] * 12,
        out_specs=[in_vmem()] * 2,
        scratch_shapes=SCRATCH + (pltpu.VMEM(state.shape, f32),),
        name="rate_two",
    )(links, counts, block_metric, inflow, plan, state_near, wall_dist, near_core(rate), *map(near_core, first), *map(near_core, second), near_core(limits))
    return tendency, step[0, 0]


def solution(mesh):
    return jax.shard_map(
        body,
        mesh=mesh,
        in_specs=(
            P("blk", None, None, None),
            P("blk", None, None),
            P("blk", None),
            P(),
            P("blk"),
            P("blk", None, None),
        ),
        out_specs=(P("blk", None, None, None), P()),
        check_vma=False,
    )
```

```python
import jax
import jax.numpy as jnp
from jax import lax
from jax.experimental import pallas as pl
from jax.experimental.pallas import tpu as pltpu
from jax.sharding import PartitionSpec as P

NI = 16
NJ = 16
NK = 16
SLOTS = 3
FIELDS = 6
LANES = 128
SPACES = 4

GAMMA = 1.4
PROD_COEF = 0.1355
DEST_COEF = 3.239
COURANT = 0.5
WALL_SIGNS = (1.0, -1.0, -1.0, -1.0, 1.0, -1.0)

SEND = (8, 8, LANES)
PLAN = 128
PLAN_I = 16
PLAN_FACE = 32
PLAN_VIA = 24

f32 = jnp.float32
i32 = jnp.int32


def iota(shape, axis):
    return lax.broadcasted_iota(i32, shape, axis)


def pick(values, index, axis):
    return jnp.take_along_axis(values, index, axis=axis, mode="promise_in_bounds")


def geometry(metric_ref, slot):
    normals = [
        [(1.0 if d == e else 0.0) + 0.25 * metric_ref[slot, 3 * d + e] for e in range(3)] for d in range(3)
    ]
    return normals, 1.0 + 0.25 * metric_ref[slot, 9]


def area_of(normal):
    total = normal[0] * normal[0] + normal[1] * normal[1] + normal[2] * normal[2]
    return jnp.sqrt(total)


def splat(value, shape):
    return jnp.full(shape, value, f32)


def primitives(cons):
    inverse = 1.0 / cons[0]
    velocity = [cons[1 + c] * inverse for c in range(3)]
    kinetic = cons[1] * velocity[0] + cons[2] * velocity[1] + cons[3] * velocity[2]
    pressure = (GAMMA - 1.0) * (cons[4] - 0.5 * kinetic)
    sound = jnp.sqrt(GAMMA * pressure * inverse)
    return inverse, velocity, pressure, sound


def fluxes_of(cons, prim, normal, area):
    _, velocity, pressure, sound = prim
    normal_vel = normal[0] * velocity[0] + normal[1] * velocity[1] + normal[2] * velocity[2]
    fluxes = [
        cons[0] * normal_vel,
        cons[1] * normal_vel + pressure * normal[0],
        cons[2] * normal_vel + pressure * normal[1],
        cons[3] * normal_vel + pressure * normal[2],
        (cons[4] + pressure) * normal_vel,
        cons[5] * normal_vel,
    ]
    return fluxes, jnp.abs(normal_vel) + sound * area


def edge(own, ghost, normal, area, sign):
    own_prim = primitives(own)
    ghost_prim = primitives(ghost)
    own_flux, own_speed = fluxes_of(own, own_prim, normal, area)
    ghost_flux, ghost_speed = fluxes_of(ghost, ghost_prim, normal, area)
    speed = sign * jnp.maximum(own_speed, ghost_speed)
    flux = [own_flux[f] + ghost_flux[f] - speed * (ghost[f] - own[f]) for f in range(FIELDS)]
    return flux, ghost_prim[1]


def split(values):
    return values[:, :LANES], values[:, LANES:]


def shifted_up(values, axis_dir):
    low, high = split(values)
    if axis_dir == 0:
        low, high = pltpu.roll(low, NI - 1, 0), pltpu.roll(high, NI - 1, 0)
    elif axis_dir == 1:
        low, high = pltpu.roll(low, LANES - NK, 1), pltpu.roll(high, LANES - NK, 1)
        low = jnp.where(iota(low.shape, 1) < LANES - NK, low, high)
    else:
        low, high = pltpu.roll(low, LANES - 1, 1), pltpu.roll(high, LANES - 1, 1)
    return jnp.concatenate([low, high], axis=1)


def shifted_down(values, axis_dir):
    low, high = split(values)
    if axis_dir == 0:
        low, high = pltpu.roll(low, 1, 0), pltpu.roll(high, 1, 0)
    elif axis_dir == 1:
        low, high = pltpu.roll(low, NK, 1), pltpu.roll(high, NK, 1)
        high = jnp.where(iota(high.shape, 1) < NK, low, high)
    else:
        low, high = pltpu.roll(low, 1, 1), pltpu.roll(high, 1, 1)
    return jnp.concatenate([low, high], axis=1)


def placed(compact, axis_dir):
    if axis_dir == 1:
        low = jnp.concatenate([compact, pltpu.roll(compact, 64, 1)], axis=0)
        high = jnp.concatenate([pltpu.roll(compact, 96, 1), pltpu.roll(compact, 32, 1)], axis=0)
        return low, high
    lane = iota((8, LANES), 1)
    index = lane // NK + jnp.where(lane % NK == NK - 1, 48, 32)
    rows = []
    for a in range(2):
        rows.append(jnp.concatenate([pick(compact, index + (64 * a + 8 * b), 1) for b in range(2)], axis=1))
    both = jnp.concatenate(rows, axis=0)
    return both, both


def put_high(values, high, axis_dir):
    if axis_dir == 0:
        return jnp.where(iota(values.shape, 0) == NI - 1, high, values)
    if axis_dir == 1:
        first, second = split(values)
        second = jnp.where(iota(second.shape, 1) >= LANES - NK, high, second)
        return jnp.concatenate([first, second], axis=1)
    return jnp.where(iota(values.shape, 1) % NK == NK - 1, high, values)


def put_low(values, low, axis_dir):
    if axis_dir == 0:
        return jnp.where(iota(values.shape, 0) == 0, low, values)
    if axis_dir == 1:
        first, second = split(values)
        first = jnp.where(iota(first.shape, 1) < NK, low, first)
        return jnp.concatenate([first, second], axis=1)
    return jnp.where(iota(values.shape, 1) % NK == 0, low, values)


def write_edges(values, slot, table_jk, table_i):
    lane = iota((8, LANES), 1)
    t = lane % NK
    group = lane // NK % 4
    index = jnp.where(
        group == 0,
        t,
        jnp.where(group == 1, LANES - NK + t, NK * (t % 8) + jnp.where(group == 3, NK - 1, 0)),
    )
    second = (group == 1) | ((group >= 2) & (t >= 8))
    for f in range(FIELDS):
        halves = []
        for a in range(2):
            rows = values[f][8 * a : 8 * a + 8]
            halves.append(jnp.where(second, pick(rows[:, LANES:], index, 1), pick(rows[:, :LANES], index, 1)))
        table_jk[slot, f] = jnp.where(lane < 64, halves[0], halves[1])
        for face in range(2):
            row = values[f][(NI - 1) * face : (NI - 1) * face + 1]
            at = 8 * (2 * slot + face) + f
            table_i[0, at : at + 1, :] = row[:, :LANES]
            table_i[1, at : at + 1, :] = row[:, LANES:]


def make_plan(links_ref, device, dev_count, plan_ref, mask_ref):
    core = device & 1
    odd_chip = lax.shift_right_logical(device, 1) & 1

    def entry(slot, face):
        code, block, other = links_ref[slot, 0, face], links_ref[slot, 1, face], links_ref[slot, 2, face]
        partner_dev = lax.div(block, SLOTS)
        away = lax.rem(partner_dev - device + dev_count, dev_count)
        space = jnp.where(
            away == 2,
            odd_chip,
            jnp.where(
                away == dev_count - 2,
                1 - odd_chip,
                jnp.where(away == 1, 2 + core, jnp.where(away == dev_count - 1, 3 - core, 4)),
            ),
        )
        space = jnp.where(code == 3, space, 4)
        return space, block - SLOTS * partner_dev, other

    for n in range(PLAN_I + 5):
        plan_ref[n] = 0
    plan_ref[PLAN_VIA] = core ^ odd_chip
    for n in range(5):
        mask_ref[n] = 0
        mask_ref[8 + n] = 0
    entries = {}
    for slot in range(SLOTS):
        for face in range(6):
            space, partner_slot, other = entry(slot, face)
            if face < 2:
                plan_ref[PLAN_I + space] = 2 * slot + face
                plan_ref[PLAN_FACE + 2 * (6 * slot + face)] = jnp.where(
                    space < 4, 2 * SLOTS + space, 2 * partner_slot + (other & 1)
                )
                continue
            count = mask_ref[8 + space]
            mask_ref[8 + space] = count + 1
            plan_ref[3 * space + jnp.where(space < 4, jnp.minimum(count, 2), 0)] = 4 * slot + face - 2
            key = 4 * partner_slot + ((other - 2) & 3)
            mask_ref[space] = mask_ref[space] | lax.shift_left(jnp.int32(1), key)
            entries[slot, face] = (space, partner_slot, key)
    for (slot, face), (space, partner_slot, key) in entries.items():
        below = mask_ref[space] & (lax.shift_left(jnp.int32(1), key) - 1)
        below = below - (lax.shift_right_logical(below, 1) & 0x555)
        below = (below & 0x333) + (lax.shift_right_logical(below, 2) & 0x333)
        below = (below + lax.shift_right_logical(below, 4)) & 0xF0F
        rank = jnp.minimum((below + lax.shift_right_logical(below, 8)) & 0xF, 2)
        at = PLAN_FACE + 2 * (6 * slot + face)
        plan_ref[at] = jnp.where(space < 4, SLOTS + space, partner_slot)
        plan_ref[at + 1] = NK * jnp.where(space < 4, rank, key & 3)


def write_sends(table_jk, table_i, plan_ref, send_refs):
    lane = iota((8, LANES), 1)
    group = lane // NK % 4
    base = (lane & 64) | (lane % NK)
    row = iota((8, LANES), 0)
    for n in range(SPACES):
        places = ((send_refs[0].at[0],), (send_refs[1].at[0],), (send_refs[2],), (send_refs[0].at[1], send_refs[1].at[1]))[n]
        chosen = []
        for q in range(3):
            source = plan_ref[3 * n + q]
            index = base + NK * (source & 3)
            slot = lax.shift_right_logical(source, 2)
            chosen.append([pick(table_jk[slot, f], index, 1) for f in range(FIELDS)])
        for f in range(FIELDS):
            value = jnp.where(group == 0, chosen[0][f], jnp.where(group == 1, chosen[1][f], chosen[2][f]))
            for place in places:
                place[f] = value
        at = pl.multiple_of(8 * plan_ref[PLAN_I + n], 8)
        first = table_i[0, pl.ds(at, 8), :]
        second = table_i[1, pl.ds(at, 8), :]
        for place in places:
            place[6] = jnp.where(row < FIELDS, first, 0.0)
            place[7] = jnp.where(row < FIELDS, second, 0.0)


def jk_ghosts(slot, table_jk, links_ref, plan_ref, far):
    lane = iota((8, LANES), 1)
    row = iota((8, LANES), 0)
    t = lane % NK
    group = lane // NK % 4
    gathered = None
    code = jnp.zeros((8, LANES), i32)
    row_index = row
    for face in range(2, 6):
        at = PLAN_FACE + 2 * (6 * slot + face)
        source, start = plan_ref[at], plan_ref[at + 1]
        orient = links_ref[slot, 3, face]
        first_rev = lax.shift_right_logical(orient, 1) & 1
        second_rev = lax.shift_right_logical(orient, 2) & 1
        index = ((lane & 64) ^ (64 * first_rev)) + (t ^ (15 * second_rev)) + start
        here = group == face - 2
        code = jnp.where(here, links_ref[slot, 0, face], code)
        row_index = jnp.where(here, row ^ (7 * first_rev), row_index)
        layers = [pick(table_jk[source, f], index, 1) for f in range(FIELDS)]
        gathered = layers if gathered is None else [jnp.where(here, new, old) for new, old in zip(layers, gathered)]
    own = [table_jk[slot, f] for f in range(FIELDS)]
    ghosts = []
    joined, distant, wall = code == 3, code == 0, code == 1
    for f in range(FIELDS):
        mirrored = own[f] if WALL_SIGNS[f] > 0 else jnp.where(wall, -own[f], own[f])
        ghosts.append(jnp.where(joined, pick(gathered[f], row_index, 0), jnp.where(distant, far[f], mirrored)))
    return own, ghosts


def i_ghosts(table_i, ghost_i, links_ref, plan_ref, far):
    row = iota((8, 2 * LANES), 0)
    flat = iota((8, 2 * LANES), 1)
    code = jnp.zeros((8, 2 * LANES), i32)
    orient = jnp.zeros((8, 2 * LANES), i32)
    for n in range(2 * SLOTS):
        slot, face = n // 2, n % 2
        at = pl.multiple_of(8 * plan_ref[PLAN_FACE + 2 * (6 * slot + face)], 8)
        for b in range(2):
            ghost_i[b, 8 * n : 8 * n + 8, :] = table_i[b, pl.ds(at, 8), :]
        code = jnp.where(row == n, links_ref[slot, 0, face], code)
        orient = jnp.where(row == n, links_ref[slot, 3, face], orient)
    first = (flat // NK) ^ (15 * ((orient >> 1) & 1))
    second = (flat % NK) ^ (15 * ((orient >> 2) & 1))
    source = jnp.where((orient & 1) == 1, NK * second + first, NK * first + second)
    upper = source >= LANES
    index = source & (LANES - 1)
    joined, distant, wall = code == 3, code == 0, code == 1
    own, ghosts = [], []
    for f in range(FIELDS):
        mine = jnp.concatenate([table_i[b, pl.ds(f, 8, stride=8), :] for b in range(2)], axis=1)
        halves = [ghost_i[b, pl.ds(f, 8, stride=8), :] for b in range(2)]
        layer = []
        for b in range(2):
            at = slice(b * LANES, (b + 1) * LANES)
            layer.append(jnp.where(upper[:, at], pick(halves[1], index[:, at], 1), pick(halves[0], index[:, at], 1)))
        layer = jnp.concatenate(layer, axis=1)
        mirrored = mine if WALL_SIGNS[f] > 0 else jnp.where(wall, -mine, mine)
        own.append(mine)
        ghosts.append(jnp.where(joined, layer, jnp.where(distant, far[f], mirrored)))
    return own, ghosts


def far_field(inflow_ref):
    density, pressure = inflow_ref[0], inflow_ref[4]
    velocity = [inflow_ref[1 + c] for c in range(3)]
    squares = velocity[0] * velocity[0] + velocity[1] * velocity[1] + velocity[2] * velocity[2]
    energy = pressure * (1.0 / (GAMMA - 1.0)) + 0.5 * density * squares
    return [density] + [density * v for v in velocity] + [energy, density * inflow_ref[5]]


def section(load, distance_ref, links_ref, counts_ref, metric_ref, inflow_ref, plan_ref, table_jk, table_i, ghost_i, edge_i, store):
    far = far_field(inflow_ref)
    own, ghosts = i_ghosts(table_i, ghost_i, links_ref, plan_ref, far)
    row = iota((8, 2 * LANES), 0)
    normal = [None] * 3
    for e in range(3):
        value = splat((1.0 if e == 0 else 0.0) + 0.25 * metric_ref[0, e], row.shape)
        for slot in range(1, SLOTS):
            value = jnp.where(row // 2 == slot, (1.0 if e == 0 else 0.0) + 0.25 * metric_ref[slot, e], value)
        normal[e] = value
    sign = jnp.where(row % 2 == 1, 1.0, -1.0)
    flux, velocity = edge(own, ghosts, normal, area_of(normal), sign)
    for n, value in enumerate(flux + velocity):
        edge_i[n] = value

    group = iota((8, LANES), 1) // NK % 4
    sign_jk = jnp.where(group % 2 == 1, 1.0, -1.0)

    def one(slot):
        normals, volume = geometry(metric_ref, slot)
        own, ghosts = jk_ghosts(slot, table_jk, links_ref, plan_ref, far)
        lane_normal = [jnp.where(group < 2, normals[1][e], normals[2][e]) for e in range(3)]
        edge_flux, edge_velocity = edge(own, ghosts, lane_normal, area_of(lane_normal), sign_jk)
        cons = load(slot)
        prim = primitives(cons)
        inverse, velocity = prim[0], prim[1]
        half_inverse = splat(0.5, (1, 1)) / splat(volume, (1, 1))
        net = [None] * FIELDS
        differences = []
        for d in range(3):
            area = area_of([splat(normals[d][e], (1, 1)) for e in range(3)])
            fluxes, speed = fluxes_of(cons, prim, normals[d], area)
            speed = jnp.maximum(speed, shifted_up(speed, d))
            for f in range(FIELDS):
                if d == 0:
                    low = edge_i[f, 2 * slot : 2 * slot + 1, :]
                    high = edge_i[f, 2 * slot + 1 : 2 * slot + 2, :]
                else:
                    low, high = placed(edge_flux[f], d)
                above = fluxes[f] + shifted_up(fluxes[f], d) - speed * (shifted_up(cons[f], d) - cons[f])
                above = put_high(above, high, d)
                change = above - put_low(shifted_down(above, d), low, d)
                net[f] = change if net[f] is None else net[f] + change
            change = []
            for c in range(3):
                if d == 0:
                    low = edge_i[FIELDS + c, 2 * slot : 2 * slot + 1, :]
                    high = edge_i[FIELDS + c, 2 * slot + 1 : 2 * slot + 2, :]
                else:
                    low, high = placed(edge_velocity[c], d)
                change.append(put_high(shifted_up(velocity[c], d), high, d) - put_low(shifted_down(velocity[c], d), low, d))
            differences.append(change)
        squares = None
        for e in range(3):
            scaled = [splat(normals[d][e], (1, 1)) * half_inverse for d in range(3)]
            for c in range(3):
                entry = scaled[0] * differences[0][c] + scaled[1] * differences[1][c] + scaled[2] * differences[2][c]
                squares = entry * entry if squares is None else squares + entry * entry
        ratio = cons[5] * inverse / distance_ref[slot]
        source = PROD_COEF * jnp.sqrt(squares) * cons[5] - DEST_COEF * cons[0] * ratio * ratio
        rates = [-net[f] * half_inverse for f in range(FIELDS)]
        rates[5] = rates[5] + source
        store(slot, cons, rates)

    for slot in range(SLOTS):
        if slot == 0:
            one(slot)
        else:
            pl.when(slot < counts_ref[0, 0])(lambda slot=slot: one(slot))


def first_kernel(dev_count, axis, links_ref, counts_ref, metric_ref, state_ref, *refs):
    send_refs, plan_ref, limits_ref = refs[:3], refs[3], refs[4]
    table_jk, table_i, mask_ref = refs[5:]
    make_plan(links_ref, lax.axis_index(axis), dev_count, plan_ref, mask_ref)
    limit = None
    for slot in range(SLOTS):
        cons = [state_ref[slot, f] for f in range(FIELDS)]
        write_edges(cons, slot, table_jk, table_i)
        normals, volume = geometry(metric_ref, slot)
        _, velocity, _, sound = primitives(cons)
        total = None
        area = None
        for d in range(3):
            normal_vel = normals[d][0] * velocity[0] + normals[d][1] * velocity[1] + normals[d][2] * velocity[2]
            total = jnp.abs(normal_vel) if total is None else total + jnp.abs(normal_vel)
            one_area = area_of([splat(normals[d][e], (1, 1)) for e in range(3)])
            area = one_area if area is None else area + one_area
        total = total + sound * area
        own = COURANT * splat(volume, (1, 1)) / jnp.max(total, axis=(0, 1), keepdims=True)
        limit = own if limit is None else jnp.where(slot < counts_ref[0, 0], jnp.minimum(limit, own), limit)
    limits_ref[...] = jnp.broadcast_to(limit, limits_ref.shape)
    write_sends(table_jk, table_i, plan_ref, send_refs)


def by_space(refs, plan_ref):
    near, far, chip, near_passed, far_passed = refs
    return [
        lambda k: near[0, k],
        lambda k: far[0, k],
        lambda k: chip[k],
        lambda k: jnp.where(plan_ref[PLAN_VIA] == 1, near_passed[1, k], far_passed[1, k]),
    ]


def fill_tables(received, table_jk, table_i):
    for n in range(SPACES):
        for f in range(FIELDS):
            table_jk[SLOTS + n, f] = received[n](f)
        for b in range(2):
            at = 8 * (2 * SLOTS + n)
            table_i[b, at : at + 8, :] = received[n](6 + b)


def second_kernel(links_ref, counts_ref, metric_ref, inflow_ref, plan_ref, state_ref, distance_ref, *refs):
    received = by_space(refs[:5], plan_ref)
    rate_ref, send_refs = refs[5], refs[6:9]
    table_jk, table_i, ghost_i, edge_i = refs[9:]
    for slot in range(SLOTS):
        write_edges([state_ref[slot, f] for f in range(FIELDS)], slot, table_jk, table_i)
    fill_tables(received, table_jk, table_i)

    def store(slot, cons, rates):
        for f in range(FIELDS):
            rate_ref[slot, f] = rates[f]

    section(
        lambda slot: [state_ref[slot, f] for f in range(FIELDS)],
        distance_ref, links_ref, counts_ref, metric_ref, inflow_ref, plan_ref, table_jk, table_i, ghost_i, edge_i, store,
    )
    for slot in range(SLOTS):
        def edges(slot=slot):
            write_edges([rate_ref[slot, f] for f in range(FIELDS)], slot, table_jk, table_i)

        if slot == 0:
            edges()
        else:
            pl.when(slot < counts_ref[0, 0])(edges)
    write_sends(table_jk, table_i, plan_ref, send_refs)


def third_kernel(links_ref, counts_ref, metric_ref, inflow_ref, plan_ref, state_ref, distance_ref, rate_ref, *refs):
    first, second, limits_ref = by_space(refs[:5], plan_ref), by_space(refs[5:10], plan_ref), refs[10]
    tendency_ref, step_ref = refs[11:13]
    table_jk, table_i, ghost_i, edge_i, middle_ref = refs[13:]
    step = jnp.min(limits_ref[...], axis=(0, 1), keepdims=True)
    step_ref[...] = step
    fill_tables([lambda k, n=n: first[n](k) + step * second[n](k) for n in range(SPACES)], table_jk, table_i)
    for slot in range(SLOTS):
        def edges(slot=slot):
            middle = [state_ref[slot, f] + step * rate_ref[slot, f] for f in range(FIELDS)]
            for f in range(FIELDS):
                middle_ref[slot, f] = middle[f]
            write_edges(middle, slot, table_jk, table_i)

        if slot == 0:
            edges()
        else:
            pl.when(slot < counts_ref[0, 0])(edges)

    def store(slot, cons, rates):
        for f in range(FIELDS):
            tendency_ref[slot, f] = 0.5 * (rate_ref[slot, f] + rates[f])

    section(
        lambda slot: [middle_ref[slot, f] for f in range(FIELDS)],
        distance_ref, links_ref, counts_ref, metric_ref, inflow_ref, plan_ref, table_jk, table_i, ghost_i, edge_i, store,
    )
    for slot in range(1, SLOTS):
        @pl.when(slot >= counts_ref[0, 0])
        def _(slot=slot):
            for f in range(FIELDS):
                tendency_ref[slot, f] = jnp.zeros((NI, NJ * NK), f32)


def in_smem():
    return pl.BlockSpec(memory_space=pltpu.SMEM)


def in_vmem():
    return pl.BlockSpec(memory_space=pltpu.VMEM)


TABLES = (
    pltpu.VMEM((SLOTS + 4, FIELDS, 8, LANES), f32),
    pltpu.VMEM((2, 8 * (2 * SLOTS + 4), LANES), f32),
)
SCRATCH = TABLES + (pltpu.VMEM((2, 64, LANES), f32), pltpu.VMEM((9, 8, 2 * LANES), f32))


def body(state, wall_dist, block_metric, inflow, counts, links):
    axis = "blk"
    dev_count = lax.axis_size(axis)
    links = jnp.transpose(links, (0, 2, 1))
    counts = counts.reshape(1, 1)
    sent = [pltpu.VMEM((2,) + SEND, f32), pltpu.VMEM((2,) + SEND, f32), pltpu.VMEM(SEND, f32)]
    block = pltpu.VMEM(state.shape, f32)

    def near_core(array):
        return pltpu.with_memory_space_constraint(array, pltpu.VMEM)

    state_near, wall_dist = near_core(state), near_core(wall_dist)

    *sends, plan, limits = pl.pallas_call(
        lambda *refs: first_kernel(dev_count, axis, *refs),
        out_shape=sent + [jax.ShapeDtypeStruct((PLAN,), i32), pltpu.VMEM((dev_count, LANES), f32)],
        in_specs=[in_smem()] * 3 + [in_vmem()],
        out_specs=[in_vmem()] * 3 + [in_smem(), in_vmem()],
        scratch_shapes=TABLES + (pltpu.SMEM((16,), i32),),
        name="faces",
    )(links, counts, block_metric, state)

    def swapped(array, other):
        return lax.ppermute(array, axis, [(p, other(p) % dev_count) for p in range(dev_count)])

    def exchanged(arrays):
        far = swapped(arrays[1], lambda p: p - 2 if p // 2 % 2 == 0 else p + 2)
        near = swapped(arrays[0], lambda p: p + 2 if p // 2 % 2 == 0 else p - 2)
        chip = swapped(arrays[2], lambda p: p ^ 1)
        near_passed = swapped(near, lambda p: p ^ 1)
        far_passed = swapped(far, lambda p: p ^ 1)
        return [near, far, chip, near_passed, far_passed]

    limits = lax.all_to_all(limits, axis, 0, 0, tiled=True)
    first = exchanged(sends)
    rate, *sends_two = pl.pallas_call(
        second_kernel,
        out_shape=[block] + sent,
        in_specs=[in_smem()] * 5 + [in_vmem()] * 7,
        out_specs=[in_vmem()] * 4,
        scratch_shapes=SCRATCH,
        name="rate_one",
    )(links, counts, block_metric, inflow, plan, state_near, wall_dist, *map(near_core, first))

    second = exchanged(sends_two)

    tendency, step = pl.pallas_call(
        third_kernel,
        out_shape=[jax.ShapeDtypeStruct(state.shape, f32), jax.ShapeDtypeStruct((1, 1), f32)],
        in_specs=[in_smem()] * 5 + [in_vmem()] * 14,
        out_specs=[in_vmem()] * 2,
        scratch_shapes=SCRATCH + (pltpu.VMEM(state.shape, f32),),
        name="rate_two",
    )(links, counts, block_metric, inflow, plan, state_near, wall_dist, near_core(rate), *map(near_core, first), *map(near_core, second), near_core(limits))
    return tendency, step[0, 0]


def solution(mesh):
    return jax.shard_map(
        body,
        mesh=mesh,
        in_specs=(
            P("blk", None, None, None),
            P("blk", None, None),
            P("blk", None),
            P(),
            P("blk"),
            P("blk", None, None),
        ),
        out_specs=(P("blk", None, None, None), P()),
        check_vma=False,
    )
```
